128 devices in a mesh: pw: 8 (over x_lo, y), pair: 16 (over z, x_hi, core).
Axes of the slice: x: 4 (x_hi: 2, x_lo: 2; x = x_hi * 2 + x_lo), y: 4, z: 4, core: 2. Of those that a mesh axis runs over, the one named last changes fastest.
Arguments:
- pair_waves: bfloat16 [16384, 16384], P('pair', 'pw'), may hold values from -6 to 6
- subspace_basis: bfloat16 [16384, 1024], P('pw'), may hold values from -0.0625 to 0.0625
- occ_band: int32 [16384], P('pair'), may hold values from 0 to 63, as said below
- empty_band: int32 [16384], P('pair'), may hold values from 0 to 255, as said below
- occ_energy: float32 [64], replicated, may hold values from -3 to -0.25
- empty_energy: float32 [256], replicated, may hold values from 0.25 to 6
- freq_grid: float32 [16], replicated, may hold values from 0.5 to 6
- freq_index: int32 [16], replicated, may hold values from 0 to 15, each once
Outputs:
- chi_tiles: float32 [16, 1024, 1024], P(None, 'pw', 'pair')
The draws below stay inside these ranges and needn't reach their ends.
Inputs may be any that keep to these rules, and one draw needn't show every extreme that they name: `freq_index`: each frequency slot names a different grid point. `occ_band`: no two pairs have the same occupied band and the same empty band. `empty_band`: no two pairs have the same occupied band and the same empty band.
All inputs are finite; a program needn't handle non-finite values.
Results may differ from the reference program's by a relative error of at most 0.017.
Values may be sent and summed in bfloat16 or wider, within the bound.
A program may use at most 64 MiB of HBM per device.

```python
import jax
import jax.numpy as jnp
from jax import lax

NPW = 16384
NB = 1024
NFREQ = 16
NOCC = 64
NEMPTY = 256
PAIRS = 16384


def pair_codes(key):
    order = jax.random.permutation(jax.random.fold_in(key, 7), NOCC * NEMPTY)
    return order[:PAIRS].astype(jnp.int32)


def draw_occ_band(key, part):
    return (pair_codes(key) // NEMPTY).astype(jnp.int32)


def draw_empty_band(key, part):
    return (pair_codes(key) % NEMPTY).astype(jnp.int32)


def spiked(result, rng, source, target, parts, factor):
    owner, partner = [(jnp.arange(result.shape[position]) // (result.shape[position] // parts)).reshape([-1 if axis == position else 1 for axis in range(result.ndim)]) for position in (source, target)]
    chosen = jax.random.permutation(rng, parts)[partner]
    strong = (owner == chosen) | (owner == (partner + parts // 2) % parts)
    return jnp.where(strong, factor * result, result)


def levels(stream_key, dims, pieces, low, top_value):
    def one(dim, shards_of):
        steps = jax.random.uniform(jax.random.fold_in(jax.random.fold_in(stream_key, 6), dim), (shards_of,), jnp.float32, low / len(pieces), top_value / len(pieces))
        return jnp.repeat(jnp.exp(steps), dims[dim] // shards_of).reshape((-1,) + (1,) * (len(dims) - dim - 1))

    level = one(*pieces[0])
    for cut in pieces[1:]:
        level = level * one(*cut)
    return level


def noise(key, extent, deviation, bound, shards=(), kind=jnp.bfloat16):
    array = deviation * jax.random.normal(key, extent, jnp.float32)
    if shards:
        array = array * levels(key, extent, shards, -0.22, 0.18)
    return jnp.clip(array, -bound, bound).astype(kind)


def heavy_noise(key, extent, spread, limit, pieces, heavy, kind=jnp.bfloat16):
    drawn = spread * jax.random.normal(key, extent, jnp.float32)
    if pieces:
        drawn = drawn * levels(key, extent, pieces, -0.22, 0.18)
    return jnp.clip(spiked(drawn, jax.random.fold_in(key, 3), *heavy), -limit, limit).astype(kind)


def setup_inputs(seed: int = 0) -> dict:
    key_of = jax.random.split(jax.random.key(seed), 9)
    return {
        "pair_waves": noise(key_of[0], (PAIRS, NPW), 1.0, 6.0, ((0, 16), (1, 8))),
        "subspace_basis": heavy_noise(key_of[1], (NPW, NB), NPW ** -0.5, 0.0625, ((0, 8),), (0, 1, 8, 2.0)),
        "occ_band": draw_occ_band(jax.random.fold_in(key_of[8], 71), 0),
        "empty_band": draw_empty_band(jax.random.fold_in(key_of[8], 71), 0),
        "occ_energy": jnp.clip(jax.random.uniform(key_of[4], (NOCC,), jnp.float32, -3.0, -0.25), -3.0, -0.25),
        "empty_energy": jnp.clip(jax.random.uniform(key_of[5], (NEMPTY,), jnp.float32, 0.25, 6.0), 0.25, 6.0),
        "freq_grid": jnp.clip(jax.random.uniform(key_of[6], (NFREQ,), jnp.float32, 0.5, 6.0), 0.5, 6.0),
        "freq_index": jax.random.permutation(key_of[7], NFREQ).astype(jnp.int32),
    }


broadening_sq = 0.0025


def lookup(indices, values_table):
    positions = jnp.arange(values_table.shape[0], dtype=jnp.int32)
    hits = indices[:, None].astype(jnp.int32) == positions[None, :]
    return jnp.sum(jnp.where(hits, values_table[None, :], jnp.zeros_like(values_table)[None, :]), axis=1)


def response(frequency, energy_gap):
    below = frequency[:, None] - energy_gap[None, :]
    above = frequency[:, None] + energy_gap[None, :]
    return below / (below * below + broadening_sq) - above / (above * above + broadening_sq)


def reference(pair_waves, subspace_basis, occ_band, empty_band, occ_energy, empty_energy, freq_grid, freq_index):
    projected = lax.dot_general(subspace_basis, pair_waves, (((0,), (1,)), ((), ())), preferred_element_type=jnp.float32).astype(jnp.bfloat16)
    energy_gap = lookup(empty_band, empty_energy) - lookup(occ_band, occ_energy)
    frequency = lookup(freq_index, freq_grid)
    prefactor = 4.0 / PAIRS
    factor = prefactor * response(frequency, energy_gap)
    projected_wide = projected.astype(jnp.float32)

    def one_frequency(freq_row):
        weighted = (projected_wide * freq_row[None, :]).astype(jnp.bfloat16)
        return lax.dot_general(weighted, projected, (((1,), (1,)), ((), ())), preferred_element_type=jnp.float32)

    return lax.map(one_frequency, factor)
```

```python
import jax
import jax.numpy as jnp
from jax import lax
from jax.experimental import pallas as pl
from jax.experimental.pallas import tpu as pltpu
from jax.sharding import PartitionSpec as P

F32, BF16 = jnp.float32, jnp.bfloat16
MESH = pl.DeviceIdType.MESH
broadening_sq = 0.0025

PAIRS = 16384
NFREQ = 16
NW = 8
NB = 1024
PL = 1024
PWL = 2048
ROWS = 128
NC = 4
CP = PL // NC
BP = CP // 4
HP = BP // 2
NQ = 4
QR = NW * ROWS // NQ
ZC = NB // 4
XC = ZC // 2


def kernel(
    occ_ref, emp_ref, pw_hbm, basis_hbm, oe_ref, ee_ref, fg_ref, fi_ref, out_ref,
    pw, basis, part, cf, acc, wt, gaps, fac,
    ta, tb, sa, sb, r1, r2, xs, xr,
    zo, zs, zt, zr, zxs, zxr, zacc, fin, finr,
    in_sem, y_send, y_recv, z_send, z_recv, c_send, c_recv,
):
    me_pw, me_pair = lax.axis_index("pw"), lax.axis_index("pair")
    y, z = me_pw % 4, me_pair // 4
    core = me_pair % 2
    y_next, y_prev, y_far = (y + 1) % 4, (y + 3) % 4, (y + 2) % 4
    z_next, z_prev, z_far = (z + 1) % 4, (z + 3) % 4, (z + 2) % 4
    x_hi = (me_pair // 2) % 2

    def along_y(t):
        return ((me_pw // 4) * 4 + t, me_pair)

    def along_z(t):
        return (me_pw, t * 4 + me_pair % 4)

    dev_yn, dev_yp = along_y(y_next), along_y(y_prev)
    dev_zn, dev_zp = along_z(z_next), along_z(z_prev)
    dev_x = ((me_pw + 4) % 8, me_pair)
    dev_xh = (me_pw, (me_pair // 4) * 4 + (me_pair + 2) % 4)
    dev_core = (me_pw, (me_pair // 2) * 2 + 1 - core)
    peers = (dev_yn, dev_yp, dev_zn, dev_zp, dev_x, dev_xh, dev_core)

    loads = [pltpu.make_async_copy(basis_hbm, basis, in_sem.at[0])]
    for c in range(NC):
        rows = pl.ds(c * CP, CP)
        loads.append(pltpu.make_async_copy(pw_hbm.at[rows], pw.at[rows], in_sem.at[1 + c]))
    for load in loads:
        load.start()

    barrier = pltpu.get_barrier_semaphore()
    for peer in peers:
        pl.semaphore_signal(barrier, inc=1, device_id=peer, device_id_type=MESH)

    sent = []

    def send(src, dst, s_sem, r_sem, dev):
        copy = pltpu.make_async_remote_copy(
            src_ref=src, dst_ref=dst, send_sem=s_sem, recv_sem=r_sem, device_id=dev, device_id_type=MESH
        )
        copy.start()
        sent.append(copy)

    def arrived(dst, sem):
        pltpu.make_async_copy(dst, dst, sem).wait()

    def quarter(t):
        return pl.multiple_of(t * BP, BP)

    def project(c):
        if c == 0:
            loads[0].wait()
        loads[1 + c].wait()

        def columns(n, carry):
            cols = pl.ds(pl.multiple_of(n * 256, 256), 256)
            part[c, :, cols] = jnp.dot(
                pw[pl.ds(c * CP, CP), :], basis[:, cols], preferred_element_type=F32
            ).astype(BF16)
            return carry

        lax.fori_loop(0, NB // 256, columns, 0)

    def y_first(c):
        far = quarter(y_far)
        send(part.at[c, pl.ds(far, HP)], ta.at[c], y_send.at[c, 0], y_recv.at[c, 0], dev_yn)
        send(part.at[c, pl.ds(far + HP, HP)], tb.at[c], y_send.at[c, 1], y_recv.at[c, 1], dev_yp)
        send(
            part.at[c, pl.ds(quarter(y_next) + HP, HP)], r1.at[c, pl.ds(HP, HP)],
            y_send.at[c, 2], y_recv.at[c, 2], dev_yn,
        )
        send(
            part.at[c, pl.ds(quarter(y_prev), HP)], r2.at[c, pl.ds(0, HP)],
            y_send.at[c, 3], y_recv.at[c, 3], dev_yp,
        )

    def y_second(c):
        arrived(ta.at[c], y_recv.at[c, 0])
        sa[c] = (ta[c].astype(F32) + part[c, pl.ds(quarter(y_next), HP), :].astype(F32)).astype(BF16)
        send(sa.at[c], r1.at[c, pl.ds(0, HP)], y_send.at[c, 4], y_recv.at[c, 4], dev_yn)
        arrived(tb.at[c], y_recv.at[c, 1])
        sb[c] = (tb[c].astype(F32) + part[c, pl.ds(quarter(y_prev) + HP, HP), :].astype(F32)).astype(BF16)
        send(sb.at[c], r2.at[c, pl.ds(HP, HP)], y_send.at[c, 5], y_recv.at[c, 5], dev_yp)

    def x_swap(c):
        arrived(r1.at[c, pl.ds(HP, HP)], y_recv.at[c, 2])
        arrived(r2.at[c, pl.ds(0, HP)], y_recv.at[c, 3])
        arrived(r1.at[c, pl.ds(0, HP)], y_recv.at[c, 4])
        arrived(r2.at[c, pl.ds(HP, HP)], y_recv.at[c, 5])
        xs[c] = (
            part[c, pl.ds(quarter(y), BP), :].astype(F32) + r1[c].astype(F32) + r2[c].astype(F32)
        ).astype(BF16)
        send(xs.at[c], xr.at[c], y_send.at[c, 6], y_recv.at[c, 6], dev_x)

    def to_core(c, start, size, k):
        send(
            cf.at[c, pl.ds(start, size)], cf.at[c, pl.ds(CP + start, size)],
            c_send.at[c, k], c_recv.at[c, k], dev_core,
        )

    def y_third(c):
        arrived(xr.at[c], y_recv.at[c, 6])
        mine = quarter(y)
        cf[c, pl.ds(mine, BP), :] = (xs[c].astype(F32) + xr[c].astype(F32)).astype(BF16)
        piece = cf.at[c, pl.ds(mine, BP)]
        send(piece, piece, y_send.at[c, 7], y_recv.at[c, 7], dev_yn)
        send(piece, piece, y_send.at[c, 8], y_recv.at[c, 8], dev_yp)
        to_core(c, mine, BP, 0)

    def y_fourth(c):
        before, after = quarter(y_prev), quarter(y_next)
        arrived(cf.at[c, pl.ds(before, BP)], y_recv.at[c, 7])
        half = cf.at[c, pl.ds(before, HP)]
        send(half, half, y_send.at[c, 9], y_recv.at[c, 9], dev_yn)
        arrived(cf.at[c, pl.ds(after, BP)], y_recv.at[c, 8])
        half = cf.at[c, pl.ds(after + HP, HP)]
        send(half, half, y_send.at[c, 10], y_recv.at[c, 10], dev_yp)
        to_core(c, before, BP, 1)
        to_core(c, after, BP, 2)

    def y_last(c):
        far = quarter(y_far)
        arrived(cf.at[c, pl.ds(far, HP)], y_recv.at[c, 9])
        arrived(cf.at[c, pl.ds(far + HP, HP)], y_recv.at[c, 10])
        to_core(c, far, BP, 3)

    def find_gaps():
        def occupied(e, value):
            return jnp.where(occ_ref[...] == e, oe_ref[e], value)

        def empty(e, value):
            return jnp.where(emp_ref[...] == e, ee_ref[e], value)

        zero = jnp.zeros((8, 128), F32)
        low = lax.fori_loop(0, 64, occupied, zero, unroll=8)
        high = lax.fori_loop(0, 256, empty, zero, unroll=8)
        gaps[0] = high - low

    def send_gaps():
        send(gaps.at[0], gaps.at[1], c_send.at[NC, 0], c_recv.at[NC, 0], dev_core)

    def find_factors():
        arrived(gaps.at[1], c_recv.at[NC, 0])
        for n in range(NW):
            frequency = fg_ref[fi_ref[core * NW + n]]
            for src in range(2):
                gap = gaps[src]
                below, above = frequency - gap, frequency + gap
                fac[src, n] = (4.0 / PAIRS) * (
                    below / (below * below + broadening_sq) - above / (above * above + broadening_sq)
                )

    def weigh(c):
        y_core = [(mine, BP, 0) for mine in (quarter(y),)]
        y_core += [(quarter(y_prev), BP, 1), (quarter(y_next), BP, 2), (quarter(y_far), BP, 3)]
        for start, size, k in y_core:
            arrived(cf.at[c, pl.ds(CP + start, size)], c_recv.at[c, k])
        rows = pl.ds(pl.multiple_of(me_pw * ROWS, ROWS), ROWS)
        for src in range(2):
            for r in range(CP // 128):
                first = src * CP + r * 128
                block = cf[c, pl.ds(first, 128), rows].astype(F32).T

                def one(n, carry):
                    row = fac[src, n, pl.ds(c * (CP // 128) + r, 1), :]
                    wt[pl.ds(pl.multiple_of(n * ROWS, ROWS), ROWS), pl.ds(first, 128)] = (
                        block * row
                    ).astype(BF16)
                    return carry

                lax.fori_loop(0, NW, one, 0, unroll=2)

    def tiles(c, q):
        rows = pl.ds(pl.multiple_of(q * QR, QR), QR)
        value = jnp.dot(wt[rows, :], cf[c], preferred_element_type=F32)
        if c:
            value = acc[rows, :] + value
        acc[rows, :] = value

    def all_tiles(c):
        def group(q, carry):
            tiles(c, q)
            return carry

        lax.fori_loop(0, NQ, group, 0)

    def zcols(t):
        return pl.ds(pl.multiple_of(t * ZC, ZC), ZC)

    def half_a(q):
        return pl.ds(q * QR, ROWS)

    def half_b(q):
        return pl.ds(q * QR + ROWS, ROWS)

    def z_first(q):
        a, b = half_a(q), half_b(q)
        zo[q, 0] = acc[a, zcols(z_far)].astype(BF16)
        send(zo.at[q, 0], zt.at[q, 0], z_send.at[q, 0], z_recv.at[q, 0], dev_zn)
        zo[q, 1] = acc[b, zcols(z_far)].astype(BF16)
        send(zo.at[q, 1], zt.at[q, 1], z_send.at[q, 1], z_recv.at[q, 1], dev_zp)
        zo[q, 2] = acc[b, zcols(z_next)].astype(BF16)
        send(zo.at[q, 2], zr.at[q, 2], z_send.at[q, 2], z_recv.at[q, 2], dev_zn)
        zo[q, 3] = acc[a, zcols(z_prev)].astype(BF16)
        send(zo.at[q, 3], zr.at[q, 3], z_send.at[q, 3], z_recv.at[q, 3], dev_zp)

    def z_second(q):
        a, b = half_a(q), half_b(q)
        arrived(zt.at[q, 0], z_recv.at[q, 0])
        zs[q, 0] = (acc[a, zcols(z_next)] + zt[q, 0].astype(F32)).astype(BF16)
        send(zs.at[q, 0], zr.at[q, 0], z_send.at[q, 4], z_recv.at[q, 4], dev_zn)
        arrived(zt.at[q, 1], z_recv.at[q, 1])
        zs[q, 1] = (acc[b, zcols(z_prev)] + zt[q, 1].astype(F32)).astype(BF16)
        send(zs.at[q, 1], zr.at[q, 1], z_send.at[q, 5], z_recv.at[q, 5], dev_zp)

    def x_last(q):
        arrived(zr.at[q, 2], z_recv.at[q, 2])
        arrived(zr.at[q, 3], z_recv.at[q, 3])
        arrived(zr.at[q, 0], z_recv.at[q, 4])
        arrived(zr.at[q, 1], z_recv.at[q, 5])
        here = pl.multiple_of(x_hi * XC, XC)
        there = pl.multiple_of((1 - x_hi) * XC, XC)
        base = pl.multiple_of(z * ZC, ZC)

        def total(half, rows, first, second, cols):
            return (
                acc[rows, pl.ds(base + cols, XC)]
                + zr[q, first, :, pl.ds(cols, XC)].astype(F32)
                + zr[q, second, :, pl.ds(cols, XC)].astype(F32)
            )

        zxs[q, 0] = total(0, half_a(q), 0, 3, there).astype(BF16)
        zxs[q, 1] = total(1, half_b(q), 2, 1, there).astype(BF16)
        send(zxs.at[q], zxr.at[q], z_send.at[q, 6], z_recv.at[q, 6], dev_xh)
        zacc[q, 0] = total(0, half_a(q), 0, 3, here)
        zacc[q, 1] = total(1, half_b(q), 2, 1, here)

    def finish(q):
        arrived(zxr.at[q], z_recv.at[q, 6])
        for h in range(2):
            fin[2 * q + h] = (zacc[q, h] + zxr[q, h].astype(F32)).T
        theirs = pl.ds(pl.multiple_of((1 - core) * 64, 64), 64)
        send(
            fin.at[pl.ds(2 * q, 2), theirs, :], finr.at[pl.ds(2 * q, 2)],
            z_send.at[q, 7], z_recv.at[q, 7], dev_core,
        )
        mine = pl.ds(pl.multiple_of(core * 64, 64), 64)
        out_ref[pl.ds(core * NW + 2 * q, 2)] = fin[pl.ds(2 * q, 2), mine, :]

    def take(q):
        arrived(finr.at[pl.ds(2 * q, 2)], z_recv.at[q, 7])
        out_ref[pl.ds((1 - core) * NW + 2 * q, 2)] = finr[pl.ds(2 * q, 2)]

    project(0)
    pl.semaphore_wait(barrier, len(peers))
    y_first(0)
    project(1)
    y_first(1)
    y_second(0)
    project(2)
    y_first(2)
    y_second(1)
    x_swap(0)
    project(3)
    y_first(3)
    y_second(2)
    x_swap(1)
    y_third(0)
    find_gaps()
    send_gaps()
    y_second(3)
    x_swap(2)
    y_third(1)
    y_fourth(0)
    find_factors()
    x_swap(3)
    y_third(2)
    y_fourth(1)
    y_last(0)
    y_third(3)
    weigh(0)
    all_tiles(0)
    y_fourth(2)
    y_last(1)
    y_fourth(3)
    weigh(1)
    all_tiles(1)
    y_last(2)
    weigh(2)
    all_tiles(2)
    y_last(3)
    weigh(3)
    for q in range(NQ):
        tiles(3, q)
        z_first(q)
        if q >= 1:
            z_second(q - 1)
        if q >= 2:
            x_last(q - 2)
    z_second(NQ - 1)
    x_last(NQ - 2)
    finish(0)
    x_last(NQ - 1)
    for q in range(1, NQ):
        finish(q)
    for q in range(NQ):
        take(q)
    for copy in sent:
        copy.wait_send()


def on_device(pair_waves, subspace_basis, occ_band, empty_band, occ_energy, empty_energy, freq_grid, freq_index):
    vmem = pl.BlockSpec(memory_space=pltpu.VMEM)
    smem = pl.BlockSpec(memory_space=pltpu.SMEM)
    hbm = pl.BlockSpec(memory_space=pl.ANY)
    dma = pltpu.SemaphoreType.DMA
    out = pl.pallas_call(
        kernel,
        out_shape=jax.ShapeDtypeStruct((NFREQ, 64, ROWS), F32),
        in_specs=[vmem, vmem, hbm, hbm, smem, smem, smem, smem],
        out_specs=vmem,
        scratch_shapes=[
            pltpu.VMEM((PL, PWL), BF16),
            pltpu.VMEM((PWL, NB), BF16),
            pltpu.VMEM((NC, CP, NB), BF16),
            pltpu.VMEM((NC, 2 * CP, NB), BF16),
            pltpu.VMEM((NW * ROWS, NB), F32),
            pltpu.VMEM((NW * ROWS, 2 * CP), BF16),
            pltpu.VMEM((2, 8, 128), F32),
            pltpu.VMEM((2, NW, 8, 128), F32),
            pltpu.VMEM((NC, HP, NB), BF16),
            pltpu.VMEM((NC, HP, NB), BF16),
            pltpu.VMEM((NC, HP, NB), BF16),
            pltpu.VMEM((NC, HP, NB), BF16),
            pltpu.VMEM((NC, BP, NB), BF16),
            pltpu.VMEM((NC, BP, NB), BF16),
            pltpu.VMEM((NC, BP, NB), BF16),
            pltpu.VMEM((NC, BP, NB), BF16),
            pltpu.VMEM((NQ, 4, ROWS, ZC), BF16),
            pltpu.VMEM((NQ, 2, ROWS, ZC), BF16),
            pltpu.VMEM((NQ, 2, ROWS, ZC), BF16),
            pltpu.VMEM((NQ, 4, ROWS, ZC), BF16),
            pltpu.VMEM((NQ, 2, ROWS, XC), BF16),
            pltpu.VMEM((NQ, 2, ROWS, XC), BF16),
            pltpu.VMEM((NQ, 2, ROWS, XC), F32),
            pltpu.VMEM((NW, ROWS, ROWS), F32),
            pltpu.VMEM((NW, 64, ROWS), F32),
            dma((1 + NC,)),
            dma((NC, 11)),
            dma((NC, 11)),
            dma((NQ, 8)),
            dma((NQ, 8)),
            dma((NC + 1, 4)),
            dma((NC + 1, 4)),
        ],
        compiler_params=pltpu.CompilerParams(collective_id=0, has_side_effects=True),
        cost_estimate=pl.CostEstimate(flops=9 << 30, bytes_accessed=9 << 20, transcendentals=0),
    )(
        occ_band.reshape(8, 128), empty_band.reshape(8, 128), pair_waves, subspace_basis,
        occ_energy, empty_energy, freq_grid, freq_index,
    )
    return jnp.swapaxes(out, 1, 2)


def solution(mesh):
    return jax.shard_map(
        on_device,
        mesh=mesh,
        in_specs=(P("pair", "pw"), P("pw", None), P("pair"), P("pair"), P(), P(), P(), P()),
        out_specs=P(None, "pw", "pair"),
        check_vma=False,
    )
```

```python
import jax
import jax.numpy as jnp
from jax import lax
from jax.experimental import pallas as pl
from jax.experimental.pallas import tpu as pltpu
from jax.sharding import PartitionSpec as P

F32, BF16 = jnp.float32, jnp.bfloat16
MESH = pl.DeviceIdType.MESH
broadening_sq = 0.0025

PAIRS = 16384
NFREQ = 16
NW = 8
NB = 1024
PL = 1024
PWL = 2048
ROWS = 128
BC = 256
NC = 8
CP = PL // NC
HP = CP // 2
NG = 4
GP = PL // NG
GC = NC // NG
NQ = 4
QR = NW * ROWS // NQ
OWN, NEXT, FAR, PREV = range(4)


def kernel(
    occ_ref, emp_ref, pw_hbm, basis_hbm, oe_ref, ee_ref, fg_ref, fi_ref, out_ref,
    pw, basis, part, cf, wt, gaps, fac,
    tab, sab, r12, xs, xr,
    val, zo, zs, zt, zr, zxs, zxr, zacc, fin, finr,
    load_sem, send_sem, y_recv, g_recv, z_recv, x_recv, c_recv,
):
    me_pw, me_pair = lax.axis_index("pw"), lax.axis_index("pair")
    x_lo, y = me_pw // 4, me_pw % 4
    z, x_hi, core = me_pair // 4, (me_pair // 2) % 2, me_pair % 2
    ys = [(y + d) % 4 for d in range(4)]
    z_next, z_prev, z_far = (z + 1) % 4, (z + 3) % 4, (z + 2) % 4

    def along_y(t):
        return (x_lo * 4 + t, me_pair)

    def along_z(t):
        return (me_pw, t * 4 + me_pair % 4)

    dev_yn, dev_yp = along_y(ys[NEXT]), along_y(ys[PREV])
    dev_zn, dev_zp = along_z(z_next), along_z(z_prev)
    dev_x = ((me_pw + 4) % 8, me_pair)
    dev_xh = (me_pw, z * 4 + (me_pair + 2) % 4)
    dev_core = (me_pw, (me_pair // 2) * 2 + 1 - core)
    peers = (dev_yn, dev_yp, dev_zn, dev_zp, dev_x, dev_xh, dev_core)

    def chunk(c):
        return pl.ds(c * CP, CP)

    def half(c, h):
        return pl.ds(c * CP + h * HP, HP)

    def group(g):
        return pl.ds(g * GP, GP)

    def group_half(g, h):
        return pl.ds(g * GP + h * (GP // 2), GP // 2)

    pw_loads = [pltpu.make_async_copy(pw_hbm.at[group(g)], pw.at[group(g)], load_sem.at[g]) for g in range(NG)]
    pw_loads[0].start()
    for d in (FAR, NEXT, PREV, OWN):
        for l in range(2):
            pltpu.make_async_copy(
                basis_hbm.at[:, pl.ds(pl.multiple_of(l * 512 + ys[d] * 128, 128), 128)],
                basis.at[ys[d], :, pl.ds(l * 128, 128)],
                load_sem.at[NG + d],
            ).start()
    for load in pw_loads[1:]:
        load.start()

    barrier = pltpu.get_barrier_semaphore()
    for peer in peers:
        pl.semaphore_signal(barrier, inc=1, device_id=peer, device_id_type=MESH)

    def remote(src, dst, s_sem, r_sem, dev):
        return pltpu.make_async_remote_copy(
            src_ref=src, dst_ref=dst, send_sem=s_sem, recv_sem=r_sem, device_id=dev, device_id_type=MESH
        )

    y_sent, c_sent, gap_sent = send_sem.at[0], send_sem.at[1], send_sem.at[2]

    def arrived(dst, sem):
        pltpu.make_async_copy(dst, dst, sem).wait()

    def project(g, d):
        if d == FAR:
            pw_loads[g].wait()
        if g == 0:
            arrived(basis.at[ys[d]], load_sem.at[NG + d])
        part[ys[d], group(g), :] = jnp.dot(
            pw[group(g), :], basis[ys[d]], preferred_element_type=F32
        ).astype(BF16)

    def chunks(g):
        return range(g * GC, (g + 1) * GC)

    def y_far(g):
        for c in chunks(g):
            remote(part.at[ys[FAR], half(c, 0)], tab.at[c, 0], y_sent, y_recv.at[c, 0], dev_yn).start()
            remote(part.at[ys[FAR], half(c, 1)], tab.at[c, 1], y_sent, y_recv.at[c, 0], dev_yp).start()

    def y_near(g):
        project(g, NEXT)
        for c in chunks(g):
            remote(
                part.at[ys[NEXT], half(c, 1)], r12.at[c, 0, pl.ds(HP, HP)], y_sent, y_recv.at[c, 1], dev_yn
            ).start()
        project(g, PREV)
        for c in chunks(g):
            remote(
                part.at[ys[PREV], half(c, 0)], r12.at[c, 1, pl.ds(0, HP)], y_sent, y_recv.at[c, 1], dev_yp
            ).start()

    def y_second(g):
        for c in chunks(g):
            arrived(tab.at[c], y_recv.at[c, 0])
            sab[c, 0] = (tab[c, 0].astype(F32) + part[ys[NEXT], half(c, 0), :].astype(F32)).astype(BF16)
            remote(sab.at[c, 0], r12.at[c, 0, pl.ds(0, HP)], y_sent, y_recv.at[c, 1], dev_yn).start()
            sab[c, 1] = (tab[c, 1].astype(F32) + part[ys[PREV], half(c, 1), :].astype(F32)).astype(BF16)
            remote(sab.at[c, 1], r12.at[c, 1, pl.ds(HP, HP)], y_sent, y_recv.at[c, 1], dev_yp).start()

    def x_swap(c):
        arrived(r12.at[c], y_recv.at[c, 1])
        xs[c] = (
            part[ys[OWN], chunk(c), :].astype(F32) + r12[c, 0].astype(F32) + r12[c, 1].astype(F32)
        ).astype(BF16)
        remote(xs.at[c], xr.at[c], y_sent, y_recv.at[c, 2], dev_x).start()

    def to_core(g, d):
        sem = c_recv.at[g] if d == OWN else c_recv.at[NG + d - 1]
        remote(cf.at[ys[d], group(g)], cf.at[ys[d], pl.ds(PL + g * GP, GP)], c_sent, sem, dev_core).start()

    def from_core(d):
        arrived(cf.at[ys[d], pl.ds(PL, PL)], c_recv.at[NG + d - 1])

    def y_third(g):
        for c in chunks(g):
            arrived(xr.at[c], y_recv.at[c, 2])
            cf[ys[OWN], chunk(c), :] = (xs[c].astype(F32) + xr[c].astype(F32)).astype(BF16)
        piece = cf.at[ys[OWN], group(g)]
        remote(piece, piece, y_sent, g_recv.at[g, 0], dev_yn).start()
        remote(piece, piece, y_sent, g_recv.at[g, 1], dev_yp).start()
        to_core(g, OWN)

    def y_fourth(g):
        arrived(cf.at[ys[PREV], group(g)], g_recv.at[g, 0])
        piece = cf.at[ys[PREV], group_half(g, 0)]
        remote(piece, piece, y_sent, g_recv.at[g, 2], dev_yn).start()
        arrived(cf.at[ys[NEXT], group(g)], g_recv.at[g, 1])
        piece = cf.at[ys[NEXT], group_half(g, 1)]
        remote(piece, piece, y_sent, g_recv.at[g, 2], dev_yp).start()
        to_core(g, PREV)
        to_core(g, NEXT)

    def y_last(g):
        arrived(cf.at[ys[FAR], group(g)], g_recv.at[g, 2])
        to_core(g, FAR)

    def find_gaps():
        def occupied(e, value):
            return jnp.where(occ_ref[...] == e, oe_ref[e], value)

        def empty(e, value):
            return jnp.where(emp_ref[...] == e, ee_ref[e], value)

        zero = jnp.zeros((8, 128), F32)
        low = lax.fori_loop(0, 64, occupied, zero, unroll=8)
        high = lax.fori_loop(0, 256, empty, zero, unroll=8)
        gaps[0] = high - low

    def send_gaps():
        remote(gaps.at[0], gaps.at[1], gap_sent, c_recv.at[NG + 3], dev_core).start()

    def find_factors():
        arrived(gaps.at[1], c_recv.at[NG + 3])
        for n in range(NW):
            frequency = fg_ref[fi_ref[core * NW + n]]
            for src in range(2):
                gap = gaps[src]
                below, above = frequency - gap, frequency + gap
                fac[src, n] = (4.0 / PAIRS) * (
                    below / (below * below + broadening_sq) - above / (above * above + broadening_sq)
                )

    def weigh(g):
        arrived(cf.at[ys[OWN], pl.ds(PL + g * GP, GP)], c_recv.at[g])
        rows = pl.ds(pl.multiple_of(x_lo * ROWS, ROWS), ROWS)
        for src in range(2):
            for r in range(GP // 128):
                first = src * PL + g * GP + r * 128
                block = cf[ys[OWN], pl.ds(first, 128), rows].astype(F32).T

                def one(n, carry):
                    row = fac[src, n, pl.ds(g * (GP // 128) + r, 1), :]
                    wt[pl.ds(pl.multiple_of(n * ROWS, ROWS), ROWS), pl.ds(first, 128)] = (
                        block * row
                    ).astype(BF16)
                    return carry

                lax.fori_loop(0, NW, one, 0, unroll=2)

    slot = [ys[d] % 2 for d in range(4)]
    root = [(z % 2) == ys[d] // 2 for d in range(4)]
    here, there = pl.ds(0, ROWS), pl.ds(ROWS, ROWS)

    def cols(t):
        return pl.ds(pl.multiple_of((t // 2) * 128, 128), 128)

    def tiles(d, q):
        val[d, q] = jnp.dot(wt[pl.ds(q * QR, QR), :], cf[ys[d]], preferred_element_type=F32)

        @pl.when(root[d])
        def _():
            zo[d, q, 0] = val[d, q, here, cols(z_far)].astype(BF16)
            remote(zo.at[d, q, 0], zt.at[slot[d], q, 0], c_sent, z_recv.at[d, q], dev_zn).start()
            zo[d, q, 1] = val[d, q, there, cols(z_far)].astype(BF16)
            remote(zo.at[d, q, 1], zt.at[slot[d], q, 1], c_sent, z_recv.at[d, q], dev_zp).start()

        @pl.when(jnp.logical_not(root[d]))
        def _():
            zo[d, q, 0] = val[d, q, there, cols(z_next)].astype(BF16)
            remote(zo.at[d, q, 0], zr.at[slot[d], q, 2], c_sent, z_recv.at[d, q], dev_zn).start()
            zo[d, q, 1] = val[d, q, here, cols(z_prev)].astype(BF16)
            remote(zo.at[d, q, 1], zr.at[slot[d], q, 3], c_sent, z_recv.at[d, q], dev_zp).start()

    def z_second(d, q):
        @pl.when(jnp.logical_not(root[d]))
        def _():
            arrived(zt.at[slot[d], q], z_recv.at[d, q])
            zs[slot[d], q, 0] = (val[d, q, here, cols(z_next)] + zt[slot[d], q, 0].astype(F32)).astype(BF16)
            remote(zs.at[slot[d], q, 0], zr.at[slot[d], q, 0], c_sent, z_recv.at[d, q], dev_zn).start()
            zs[slot[d], q, 1] = (val[d, q, there, cols(z_prev)] + zt[slot[d], q, 1].astype(F32)).astype(BF16)
            remote(zs.at[slot[d], q, 1], zr.at[slot[d], q, 1], c_sent, z_recv.at[d, q], dev_zp).start()

    def z_third(d, q):
        @pl.when(root[d])
        def _():
            arrived(zr.at[slot[d], q], z_recv.at[d, q])

            def total(rows, first, second):
                return (
                    val[d, q, rows, cols(z)]
                    + zr[slot[d], q, first].astype(F32)
                    + zr[slot[d], q, second].astype(F32)
                )

            @pl.when(slot[d] == x_hi)
            def _():
                zacc[q, 0] = total(here, 0, 3)
                zacc[q, 1] = total(there, 2, 1)

            @pl.when(slot[d] != x_hi)
            def _():
                zxs[q, 0] = total(here, 0, 3).astype(BF16)
                zxs[q, 1] = total(there, 2, 1).astype(BF16)
                remote(zxs.at[q], zxr.at[q], c_sent, x_recv.at[q, 0], dev_xh).start()

    def finish(q):
        arrived(zxr.at[q], x_recv.at[q, 0])
        for h in range(2):
            fin[2 * q + h] = (zacc[q, h] + zxr[q, h].astype(F32)).T
        theirs = pl.ds(pl.multiple_of((1 - core) * 64, 64), 64)
        remote(
            fin.at[pl.ds(2 * q, 2), theirs, :], finr.at[pl.ds(2 * q, 2)], c_sent, x_recv.at[q, 1], dev_core
        ).start()
        mine = pl.ds(pl.multiple_of(core * 64, 64), 64)
        out_ref[pl.ds(core * NW + 2 * q, 2)] = fin[pl.ds(2 * q, 2), mine, :]

    def take(q):
        arrived(finr.at[pl.ds(2 * q, 2)], x_recv.at[q, 1])
        out_ref[pl.ds((1 - core) * NW + 2 * q, 2)] = finr[pl.ds(2 * q, 2)]

    project(0, FAR)
    pl.semaphore_wait(barrier, len(peers))
    y_far(0)
    project(1, FAR)
    y_far(1)
    y_near(0)
    y_second(0)
    project(2, FAR)
    y_far(2)
    y_near(1)
    y_second(1)
    project(3, FAR)
    y_far(3)
    y_near(2)
    project(0, OWN)
    x_swap(0)
    x_swap(1)
    y_second(2)
    y_near(3)
    project(1, OWN)
    x_swap(2)
    x_swap(3)
    project(2, OWN)
    y_second(3)
    y_third(0)
    project(3, OWN)
    find_gaps()
    send_gaps()
    x_swap(4)
    x_swap(5)
    y_third(1)
    find_factors()
    weigh(0)
    x_swap(6)
    x_swap(7)
    y_third(2)
    weigh(1)
    y_third(3)
    weigh(2)
    weigh(3)
    y_fourth(0)
    y_fourth(1)
    for q in range(NQ):
        tiles(OWN, q)
    y_fourth(2)
    y_fourth(3)
    from_core(NEXT)
    for q in range(NQ):
        z_second(OWN, q)
        tiles(NEXT, q)
    from_core(PREV)
    y_last(0)
    y_last(1)
    for q in range(NQ):
        z_third(OWN, q)
        z_second(NEXT, q)
        tiles(PREV, q)
    y_last(2)
    y_last(3)
    from_core(FAR)
    for q in range(NQ):
        z_second(PREV, q)
        tiles(FAR, q)
    for q in range(NQ):
        z_third(NEXT, q)
    for q in range(NQ):
        z_second(FAR, q)
        z_third(PREV, q)
    for q in range(NQ):
        z_third(FAR, q)
    for q in range(NQ):
        finish(q)
    for q in range(NQ):
        take(q)
    arrived(pw.at[pl.ds(0, 896)], y_sent)
    arrived(pw, c_sent)
    arrived(gaps.at[0], gap_sent)


def on_device(pair_waves, subspace_basis, occ_band, empty_band, occ_energy, empty_energy, freq_grid, freq_index):
    vmem = pl.BlockSpec(memory_space=pltpu.VMEM)
    smem = pl.BlockSpec(memory_space=pltpu.SMEM)
    hbm = pl.BlockSpec(memory_space=pl.ANY)
    dma = pltpu.SemaphoreType.DMA
    out = pl.pallas_call(
        kernel,
        out_shape=jax.ShapeDtypeStruct((NFREQ, 64, ROWS), F32),
        in_specs=[vmem, vmem, hbm, hbm, smem, smem, smem, smem],
        out_specs=vmem,
        scratch_shapes=[
            pltpu.VMEM((PL, PWL), BF16),
            pltpu.VMEM((4, PWL, BC), BF16),
            pltpu.VMEM((4, PL, BC), BF16),
            pltpu.VMEM((4, 2 * PL, BC), BF16),
            pltpu.VMEM((NW * ROWS, 2 * PL), BF16),
            pltpu.VMEM((2, 8, 128), F32),
            pltpu.VMEM((2, NW, 8, 128), F32),
            pltpu.VMEM((NC, 2, HP, BC), BF16),
            pltpu.VMEM((NC, 2, HP, BC), BF16),
            pltpu.VMEM((NC, 2, CP, BC), BF16),
            pltpu.VMEM((NC, CP, BC), BF16),
            pltpu.VMEM((NC, CP, BC), BF16),
            pltpu.VMEM((4, NQ, QR, BC), F32),
            pltpu.VMEM((4, NQ, 2, ROWS, ROWS), BF16),
            pltpu.VMEM((2, NQ, 2, ROWS, ROWS), BF16),
            pltpu.VMEM((2, NQ, 2, ROWS, ROWS), BF16),
            pltpu.VMEM((2, NQ, 4, ROWS, ROWS), BF16),
            pltpu.VMEM((NQ, 2, ROWS, ROWS), BF16),
            pltpu.VMEM((NQ, 2, ROWS, ROWS), BF16),
            pltpu.VMEM((NQ, 2, ROWS, ROWS), F32),
            pltpu.VMEM((NW, ROWS, ROWS), F32),
            pltpu.VMEM((NW, 64, ROWS), F32),
            dma((NG + 4,)),
            dma((3,)),
            dma((NC, 3)),
            dma((NG, 3)),
            dma((4, NQ)),
            dma((NQ, 2)),
            dma((NG + 4,)),
        ],
        compiler_params=pltpu.CompilerParams(collective_id=0, has_side_effects=True),
        cost_estimate=pl.CostEstimate(flops=9 << 30, bytes_accessed=9 << 20, transcendentals=0),
    )(
        occ_band.reshape(8, 128), empty_band.reshape(8, 128), pair_waves, subspace_basis,
        occ_energy, empty_energy, freq_grid, freq_index,
    )
    return jnp.swapaxes(out, 1, 2)


def solution(mesh):
    return jax.shard_map(
        on_device,
        mesh=mesh,
        in_specs=(P("pair", "pw"), P("pw", None), P("pair"), P("pair"), P(), P(), P(), P()),
        out_specs=P(None, "pw", "pair"),
        check_vma=False,
    )
```

```python
import jax
import jax.numpy as jnp
from jax import lax
from jax.experimental import pallas as pl
from jax.experimental.pallas import tpu as pltpu
from jax.sharding import PartitionSpec as P

F32, BF16 = jnp.float32, jnp.bfloat16
MESH = pl.DeviceIdType.MESH
broadening_sq = 0.0025

PAIRS = 16384
NFREQ = 16
NW = 8
NB = 1024
PL = 1024
PWL = 2048
ROWS = 128
BC = 256
NC = 8
CP = PL // NC
HP = CP // 2
NG = 4
GP = PL // NG
GC = NC // NG
NQ = 4
QR = NW * ROWS // NQ
OWN, NEXT, FAR, PREV = range(4)


def kernel(
    occ_ref, emp_ref, pw_hbm, basis_hbm, oe_ref, ee_ref, fg_ref, fi_ref, out_ref,
    pw, basis, part, cf, wt, gaps, fac,
    hx, hs, tab, sab, r12, xs, xr,
    val, zo, zs, zt, zr, zxs, zxr, fin, finr,
    load_sem, send_sem, y_recv, g_recv, h_recv, z_recv, x_recv, c_recv,
):
    me_pw, me_pair = lax.axis_index("pw"), lax.axis_index("pair")
    x_lo, y = me_pw // 4, me_pw % 4
    z, x_hi, core = me_pair // 4, (me_pair // 2) % 2, me_pair % 2
    ys = [(y + d) % 4 for d in range(4)]
    z_next, z_prev, z_far = (z + 1) % 4, (z + 3) % 4, (z + 2) % 4

    def along_y(t):
        return (x_lo * 4 + t, me_pair)

    def along_z(t):
        return (me_pw, t * 4 + me_pair % 4)

    dev_yn, dev_yp = along_y(ys[NEXT]), along_y(ys[PREV])
    dev_zn, dev_zp = along_z(z_next), along_z(z_prev)
    dev_x = ((me_pw + 4) % 8, me_pair)
    dev_xh = (me_pw, z * 4 + (me_pair + 2) % 4)
    dev_xhc = (me_pw, z * 4 + ((me_pair // 2) * 2 + 3 - core) % 4)
    dev_core = (me_pw, (me_pair // 2) * 2 + 1 - core)
    peers = (dev_yn, dev_yp, dev_zn, dev_zp, dev_x, dev_xh, dev_xhc, dev_core)

    def chunk(c):
        return pl.ds(c * CP, CP)

    def half(c, h):
        return pl.ds(c * CP + h * HP, HP)

    def group(g):
        return pl.ds(g * GP, GP)

    def group_half(g, h):
        return pl.ds(g * GP + h * (GP // 2), GP // 2)

    pw_loads = [pltpu.make_async_copy(pw_hbm.at[group(g)], pw.at[group(g)], load_sem.at[g]) for g in range(NG)]
    def load_basis(d):
        for l in range(2):
            pltpu.make_async_copy(
                basis_hbm.at[:, pl.ds(pl.multiple_of(l * 512 + ys[d] * 128, 128), 128)],
                basis.at[ys[d], :, pl.ds(l * 128, 128)],
                load_sem.at[NG + d],
            ).start()

    load_basis(FAR)
    pw_loads[1].start()
    pw_loads[0].start()
    load_basis(NEXT)
    load_basis(PREV)
    pw_loads[2].start()
    pw_loads[3].start()
    load_basis(OWN)

    barrier = pltpu.get_barrier_semaphore()
    for peer in peers:
        pl.semaphore_signal(barrier, inc=1, device_id=peer, device_id_type=MESH)

    def remote(src, dst, s_sem, r_sem, dev):
        return pltpu.make_async_remote_copy(
            src_ref=src, dst_ref=dst, send_sem=s_sem, recv_sem=r_sem, device_id=dev, device_id_type=MESH
        )

    y_sent, c_sent, gap_sent = send_sem.at[0], send_sem.at[1], send_sem.at[2]

    def arrived(dst, sem):
        pltpu.make_async_copy(dst, dst, sem).wait()

    def project(g, d):
        if d == FAR:
            pw_loads[g].wait()
        if g == 1:
            arrived(basis.at[ys[d]], load_sem.at[NG + d])
        part[ys[d], group(g), :] = jnp.dot(
            pw[group(g), :], basis[ys[d]], preferred_element_type=F32
        ).astype(BF16)

    def chunks(g):
        return range(g * GC, (g + 1) * GC)

    def mine(c, d):
        return hs.at[ys[d]] if c == 0 else part.at[ys[d], chunk(c)]

    kept = pl.ds(pl.multiple_of(x_lo * CP, CP), CP)
    given = pl.ds(pl.multiple_of((1 - x_lo) * CP, CP), CP)

    def x_give(d):
        project(0, d)
        remote(part.at[ys[d], given], hx.at[ys[d]], y_sent, h_recv.at[0, d], dev_x).start()

    def x_take(d):
        arrived(hx.at[ys[d]], h_recv.at[0, d])
        hs[ys[d]] = (part[ys[d], kept, :].astype(F32) + hx[ys[d]].astype(F32)).astype(BF16)

    low, high = pl.ds(0, HP), pl.ds(HP, HP)

    def y_far(c):
        remote(mine(c, FAR).at[low], tab.at[c, 0], y_sent, y_recv.at[c, 0], dev_yn).start()
        remote(mine(c, FAR).at[high], tab.at[c, 1], y_sent, y_recv.at[c, 0], dev_yp).start()

    def y_next_half(c):
        remote(mine(c, NEXT).at[high], r12.at[c, 0, high], y_sent, y_recv.at[c, 1], dev_yn).start()

    def y_prev_half(c):
        remote(mine(c, PREV).at[low], r12.at[c, 1, low], y_sent, y_recv.at[c, 1], dev_yp).start()

    def y_second(c):
        arrived(tab.at[c], y_recv.at[c, 0])
        sab[c, 0] = (tab[c, 0].astype(F32) + mine(c, NEXT)[low, :].astype(F32)).astype(BF16)
        remote(sab.at[c, 0], r12.at[c, 0, low], y_sent, y_recv.at[c, 1], dev_yn).start()
        sab[c, 1] = (tab[c, 1].astype(F32) + mine(c, PREV)[high, :].astype(F32)).astype(BF16)
        remote(sab.at[c, 1], r12.at[c, 1, high], y_sent, y_recv.at[c, 1], dev_yp).start()

    def y_total(c):
        arrived(r12.at[c], y_recv.at[c, 1])
        return (mine(c, OWN)[...].astype(F32) + r12[c, 0].astype(F32) + r12[c, 1].astype(F32)).astype(BF16)

    def x_swap(c):
        xs[c] = y_total(c)
        remote(xs.at[c], xr.at[c], y_sent, y_recv.at[c, 2], dev_x).start()

    def group_far(g):
        project(g, FAR)
        for c in chunks(g):
            y_far(c)

    def group_near(g):
        project(g, NEXT)
        for c in chunks(g):
            y_next_half(c)
        project(g, PREV)
        for c in chunks(g):
            y_prev_half(c)

    def group_second(g):
        for c in chunks(g):
            y_second(c)

    def group_swap(g):
        for c in chunks(g):
            x_swap(c)

    def first_far():
        x_take(FAR)
        y_far(0)

    def first_near():
        x_take(NEXT)
        y_next_half(0)
        x_take(PREV)
        y_prev_half(0)

    def x_share(d):
        piece = cf.at[ys[d], kept]
        remote(piece, piece, y_sent, h_recv.at[1, d], dev_x).start()

    def x_shared(d):
        arrived(cf.at[ys[d], given], h_recv.at[1, d])
        to_core(0, d)

    def first_third():
        x_take(OWN)
        cf[ys[OWN], kept, :] = y_total(0)
        piece = cf.at[ys[OWN], kept]
        remote(piece, piece, y_sent, g_recv.at[0, 0], dev_yn).start()
        remote(piece, piece, y_sent, g_recv.at[0, 1], dev_yp).start()
        x_share(OWN)

    def kept_half(h):
        return pl.ds(pl.multiple_of(x_lo * CP + h * HP, HP), HP)

    def first_fourth():
        arrived(cf.at[ys[PREV], kept], g_recv.at[0, 0])
        piece = cf.at[ys[PREV], kept_half(0)]
        remote(piece, piece, y_sent, g_recv.at[0, 2], dev_yn).start()
        x_share(PREV)
        arrived(cf.at[ys[NEXT], kept], g_recv.at[0, 1])
        piece = cf.at[ys[NEXT], kept_half(1)]
        remote(piece, piece, y_sent, g_recv.at[0, 2], dev_yp).start()
        x_share(NEXT)

    def first_last():
        arrived(cf.at[ys[FAR], kept], g_recv.at[0, 2])
        x_share(FAR)

    def to_core(g, d):
        sem = c_recv.at[g] if d == OWN else c_recv.at[NG + d - 1]
        remote(cf.at[ys[d], group(g)], cf.at[ys[d], pl.ds(PL + g * GP, GP)], c_sent, sem, dev_core).start()

    def from_core(d):
        arrived(cf.at[ys[d], pl.ds(PL, PL)], c_recv.at[NG + d - 1])

    def y_third(g):
        for c in chunks(g):
            arrived(xr.at[c], y_recv.at[c, 2])
            cf[ys[OWN], chunk(c), :] = (xs[c].astype(F32) + xr[c].astype(F32)).astype(BF16)
        piece = cf.at[ys[OWN], group(g)]
        remote(piece, piece, y_sent, g_recv.at[g, 0], dev_yn).start()
        remote(piece, piece, y_sent, g_recv.at[g, 1], dev_yp).start()
        to_core(g, OWN)

    def y_fourth(g):
        arrived(cf.at[ys[PREV], group(g)], g_recv.at[g, 0])
        piece = cf.at[ys[PREV], group_half(g, 0)]
        remote(piece, piece, y_sent, g_recv.at[g, 2], dev_yn).start()
        arrived(cf.at[ys[NEXT], group(g)], g_recv.at[g, 1])
        piece = cf.at[ys[NEXT], group_half(g, 1)]
        remote(piece, piece, y_sent, g_recv.at[g, 2], dev_yp).start()
        to_core(g, PREV)
        to_core(g, NEXT)

    def y_last(g):
        arrived(cf.at[ys[FAR], group(g)], g_recv.at[g, 2])
        to_core(g, FAR)

    def find_gaps():
        def occupied(e, value):
            return jnp.where(occ_ref[...] == e, oe_ref[e], value)

        def empty(e, value):
            return jnp.where(emp_ref[...] == e, ee_ref[e], value)

        zero = jnp.zeros((8, 128), F32)
        below = lax.fori_loop(0, 64, occupied, zero, unroll=8)
        above = lax.fori_loop(0, 256, empty, zero, unroll=8)
        gaps[0] = above - below

    def send_gaps():
        remote(gaps.at[0], gaps.at[1], gap_sent, c_recv.at[NG + 3], dev_core).start()

    def find_factors():
        arrived(gaps.at[1], c_recv.at[NG + 3])
        for n in range(NW):
            frequency = fg_ref[fi_ref[core * NW + n]]
            for src in range(2):
                gap = gaps[src]
                below, above = frequency - gap, frequency + gap
                fac[src, n] = (4.0 / PAIRS) * (
                    below / (below * below + broadening_sq) - above / (above * above + broadening_sq)
                )

    def weigh(g):
        arrived(cf.at[ys[OWN], pl.ds(PL + g * GP, GP)], c_recv.at[g])
        rows = pl.ds(pl.multiple_of(x_lo * ROWS, ROWS), ROWS)
        for src in range(2):
            for r in range(GP // 128):
                first = src * PL + g * GP + r * 128
                block = cf[ys[OWN], pl.ds(first, 128), rows].astype(F32).T

                def one(n, carry):
                    row = fac[src, n, pl.ds(g * (GP // 128) + r, 1), :]
                    wt[pl.ds(pl.multiple_of(n * ROWS, ROWS), ROWS), pl.ds(first, 128)] = (
                        block * row
                    ).astype(BF16)
                    return carry

                lax.fori_loop(0, NW, one, 0, unroll=2)

    slot = [ys[d] % 2 for d in range(4)]
    root = [(z % 2) == ys[d] // 2 for d in range(4)]
    here, there = pl.ds(0, ROWS), pl.ds(ROWS, ROWS)

    def cols(t):
        return pl.ds(pl.multiple_of((t // 2) * 128, 128), 128)

    def tiles(d, q):
        val[d, q] = jnp.dot(wt[pl.ds(q * QR, QR), :], cf[ys[d]], preferred_element_type=F32)

        @pl.when(root[d])
        def _():
            zo[d, q, 0] = val[d, q, here, cols(z_far)].astype(BF16)
            remote(zo.at[d, q, 0], zt.at[slot[d], q, 0], c_sent, z_recv.at[d, q], dev_zn).start()
            zo[d, q, 1] = val[d, q, there, cols(z_far)].astype(BF16)
            remote(zo.at[d, q, 1], zt.at[slot[d], q, 1], c_sent, z_recv.at[d, q], dev_zp).start()

        @pl.when(jnp.logical_not(root[d]))
        def _():
            zo[d, q, 0] = val[d, q, there, cols(z_next)].astype(BF16)
            remote(zo.at[d, q, 0], zr.at[slot[d], q, 2], c_sent, z_recv.at[d, q], dev_zn).start()
            zo[d, q, 1] = val[d, q, here, cols(z_prev)].astype(BF16)
            remote(zo.at[d, q, 1], zr.at[slot[d], q, 3], c_sent, z_recv.at[d, q], dev_zp).start()

    def z_second(d, q):
        @pl.when(jnp.logical_not(root[d]))
        def _():
            arrived(zt.at[slot[d], q], z_recv.at[d, q])
            zs[slot[d], q, 0] = (val[d, q, here, cols(z_next)] + zt[slot[d], q, 0].astype(F32)).astype(BF16)
            remote(zs.at[slot[d], q, 0], zr.at[slot[d], q, 0], c_sent, z_recv.at[d, q], dev_zn).start()
            zs[slot[d], q, 1] = (val[d, q, there, cols(z_prev)] + zt[slot[d], q, 1].astype(F32)).astype(BF16)
            remote(zs.at[slot[d], q, 1], zr.at[slot[d], q, 1], c_sent, z_recv.at[d, q], dev_zp).start()

    ours = pl.ds(pl.multiple_of(core * 64, 64), 64)
    theirs = pl.ds(pl.multiple_of((1 - core) * 64, 64), 64)

    def z_third(d, q):
        @pl.when(root[d])
        def _():
            arrived(zr.at[slot[d], q], z_recv.at[d, q])

            def total(rows, first, second):
                return (
                    val[d, q, rows, cols(z)]
                    + zr[slot[d], q, first].astype(F32)
                    + zr[slot[d], q, second].astype(F32)
                ).T

            @pl.when(slot[d] == x_hi)
            def _():
                fin[2 * q] = total(here, 0, 3)
                fin[2 * q + 1] = total(there, 2, 1)
                remote(
                    fin.at[pl.ds(2 * q, 2), theirs, :], finr.at[pl.ds(2 * q, 2)], c_sent, x_recv.at[q, 2], dev_core
                ).start()

            @pl.when(slot[d] != x_hi)
            def _():
                zxs[q, 0] = total(here, 0, 3).astype(BF16)
                zxs[q, 1] = total(there, 2, 1).astype(BF16)
                remote(zxs.at[q, :, ours, :], zxr.at[q, 0], c_sent, x_recv.at[q, 0], dev_xh).start()
                remote(zxs.at[q, :, theirs, :], zxr.at[q, 1], c_sent, x_recv.at[q, 1], dev_xhc).start()

    def finish(q):
        arrived(zxr.at[q, 0], x_recv.at[q, 0])
        out_ref[pl.ds(core * NW + 2 * q, 2)] = fin[pl.ds(2 * q, 2), ours, :] + zxr[q, 0].astype(F32)
        arrived(finr.at[pl.ds(2 * q, 2)], x_recv.at[q, 2])
        arrived(zxr.at[q, 1], x_recv.at[q, 1])
        out_ref[pl.ds((1 - core) * NW + 2 * q, 2)] = finr[pl.ds(2 * q, 2)] + zxr[q, 1].astype(F32)

    project(1, FAR)
    pl.semaphore_wait(barrier, len(peers))
    y_far(2)
    y_far(3)
    x_give(FAR)
    group_far(2)
    group_near(1)
    x_give(NEXT)
    group_second(1)
    x_give(PREV)
    group_far(3)
    first_far()
    group_near(2)
    group_second(2)
    project(1, OWN)
    first_near()
    group_swap(1)
    x_give(OWN)
    group_near(3)
    y_second(0)
    group_second(3)
    project(2, OWN)
    find_gaps()
    send_gaps()
    group_swap(2)
    project(3, OWN)
    first_third()
    y_third(1)
    group_swap(3)
    find_factors()
    y_third(2)
    x_shared(OWN)
    weigh(1)
    first_fourth()
    y_third(3)
    weigh(2)
    weigh(0)
    y_fourth(1)
    weigh(3)
    tiles(OWN, 0)
    y_fourth(2)
    tiles(OWN, 1)
    tiles(OWN, 2)
    z_second(OWN, 0)
    tiles(OWN, 3)
    x_shared(PREV)
    x_shared(NEXT)
    y_fourth(3)
    first_last()
    for q in range(1, NQ):
        z_second(OWN, q)
    from_core(NEXT)
    for q in range(NQ):
        tiles(NEXT, q)
    x_shared(FAR)
    y_last(1)
    from_core(PREV)
    for q in range(NQ):
        tiles(PREV, q)
        z_third(OWN, q)
        z_second(NEXT, q)
        if q < 2:
            y_last(q + 2)
    from_core(FAR)
    for q in range(NQ):
        z_second(PREV, q)
        tiles(FAR, q)
    for q in range(NQ):
        z_third(NEXT, q)
    for q in range(NQ):
        z_second(FAR, q)
        z_third(PREV, q)
    for q in range(NQ):
        z_third(FAR, q)
    for q in range(NQ):
        finish(q)
    arrived(pw.at[pl.ds(0, 896)], y_sent)
    arrived(pw, c_sent)
    arrived(gaps.at[0], gap_sent)


def on_device(pair_waves, subspace_basis, occ_band, empty_band, occ_energy, empty_energy, freq_grid, freq_index):
    vmem = pl.BlockSpec(memory_space=pltpu.VMEM)
    smem = pl.BlockSpec(memory_space=pltpu.SMEM)
    hbm = pl.BlockSpec(memory_space=pltpu.HBM)
    dma = pltpu.SemaphoreType.DMA
    out = pl.pallas_call(
        kernel,
        out_shape=jax.ShapeDtypeStruct((NFREQ, 64, ROWS), F32),
        in_specs=[vmem, vmem, hbm, hbm, smem, smem, smem, smem],
        out_specs=vmem,
        scratch_shapes=[
            pltpu.VMEM((PL, PWL), BF16),
            pltpu.VMEM((4, PWL, BC), BF16),
            pltpu.VMEM((4, PL, BC), BF16),
            pltpu.VMEM((4, 2 * PL, BC), BF16),
            pltpu.VMEM((NW * ROWS, 2 * PL), BF16),
            pltpu.VMEM((2, 8, 128), F32),
            pltpu.VMEM((2, NW, 8, 128), F32),
            pltpu.VMEM((4, CP, BC), BF16),
            pltpu.VMEM((4, CP, BC), BF16),
            pltpu.VMEM((NC, 2, HP, BC), BF16),
            pltpu.VMEM((NC, 2, HP, BC), BF16),
            pltpu.VMEM((NC, 2, CP, BC), BF16),
            pltpu.VMEM((NC, CP, BC), BF16),
            pltpu.VMEM((NC, CP, BC), BF16),
            pltpu.VMEM((4, NQ, QR, BC), F32),
            pltpu.VMEM((4, NQ, 2, ROWS, ROWS), BF16),
            pltpu.VMEM((2, NQ, 2, ROWS, ROWS), BF16),
            pltpu.VMEM((2, NQ, 2, ROWS, ROWS), BF16),
            pltpu.VMEM((2, NQ, 4, ROWS, ROWS), BF16),
            pltpu.VMEM((NQ, 2, ROWS, ROWS), BF16),
            pltpu.VMEM((NQ, 2, 2, 64, ROWS), BF16),
            pltpu.VMEM((NW, ROWS, ROWS), F32),
            pltpu.VMEM((NW, 64, ROWS), F32),
            dma((NG + 4,)),
            dma((3,)),
            dma((NC, 3)),
            dma((NG, 3)),
            dma((2, 4)),
            dma((4, NQ)),
            dma((NQ, 3)),
            dma((NG + 4,)),
        ],
        compiler_params=pltpu.CompilerParams(collective_id=0, has_side_effects=True, vmem_limit_bytes=48 << 20),
        cost_estimate=pl.CostEstimate(flops=9 << 30, bytes_accessed=9 << 20, transcendentals=0),
    )(
        *(
            pltpu.with_memory_space_constraint(array, pltpu.HBM)
            for array in (
                occ_band.reshape(8, 128), empty_band.reshape(8, 128), pair_waves, subspace_basis,
                occ_energy, empty_energy, freq_grid, freq_index,
            )
        )
    )
    return jnp.swapaxes(out, 1, 2)


def solution(mesh):
    return jax.shard_map(
        on_device,
        mesh=mesh,
        in_specs=(P("pair", "pw"), P("pw", None), P("pair"), P("pair"), P(), P(), P(), P()),
        out_specs=P(None, "pw", "pair"),
        check_vma=False,
    )
```

```python
import jax
import jax.numpy as jnp
from jax import lax
from jax.experimental import pallas as pl
from jax.experimental.pallas import tpu as pltpu
from jax.sharding import PartitionSpec as P

F32, BF16 = jnp.float32, jnp.bfloat16
MESH = pl.DeviceIdType.MESH
broadening_sq = 0.0025

PAIRS = 16384
NFREQ = 16
NW = 8
NB = 1024
PL = 1024
PWL = 2048
ROWS = 128
BC = 256
NC = 8
CP = PL // NC
HP = CP // 2
NG = 4
GP = PL // NG
GC = NC // NG
NQ = 4
QR = NW * ROWS // NQ
OWN, NEXT, FAR, PREV = range(4)


def kernel(
    occ_hbm, emp_hbm, pw_hbm, basis_hbm, oe_hbm, ee_hbm, fg_hbm, fi_hbm, out_ref,
    occ_ref, emp_ref, oe_ref, ee_ref, fg_ref, fi_ref,
    pw, basis, part, cf, wt, gaps, fac,
    hx, hs, tab, sab, r12, xs, xr,
    val, zo, zs, zt, zr, zxs, zxr, fin, finr,
    load_sem, small_sem, send_sem, y_recv, g_recv, h_recv, z_recv, x_recv, c_recv,
):
    me_pw, me_pair = lax.axis_index("pw"), lax.axis_index("pair")
    x_lo, y = me_pw // 4, me_pw % 4
    z, x_hi, core = me_pair // 4, (me_pair // 2) % 2, me_pair % 2
    ys = [(y + d) % 4 for d in range(4)]
    z_next, z_prev, z_far = (z + 1) % 4, (z + 3) % 4, (z + 2) % 4

    def along_y(t):
        return (x_lo * 4 + t, me_pair)

    def along_z(t):
        return (me_pw, t * 4 + me_pair % 4)

    dev_yn, dev_yp = along_y(ys[NEXT]), along_y(ys[PREV])
    dev_zn, dev_zp = along_z(z_next), along_z(z_prev)
    dev_x = ((me_pw + 4) % 8, me_pair)
    dev_xh = (me_pw, z * 4 + (me_pair + 2) % 4)
    dev_xhc = (me_pw, z * 4 + ((me_pair // 2) * 2 + 3 - core) % 4)
    dev_core = (me_pw, (me_pair // 2) * 2 + 1 - core)
    peers = (dev_yn, dev_yp, dev_zn, dev_zp, dev_x, dev_xh, dev_xhc, dev_core)

    def chunk(c):
        return pl.ds(c * CP, CP)

    def half(c, h):
        return pl.ds(c * CP + h * HP, HP)

    def group(g):
        return pl.ds(g * GP, GP)

    def group_half(g, h):
        return pl.ds(g * GP + h * (GP // 2), GP // 2)

    pw_loads = [pltpu.make_async_copy(pw_hbm.at[group(g)], pw.at[group(g)], load_sem.at[g]) for g in range(NG)]
    def load_basis(d):
        for l in range(2):
            pltpu.make_async_copy(
                basis_hbm.at[:, pl.ds(pl.multiple_of(l * 512 + ys[d] * 128, 128), 128)],
                basis.at[ys[d], :, pl.ds(l * 128, 128)],
                load_sem.at[NG + d],
            ).start()

    load_basis(FAR)
    pw_loads[1].start()
    pw_loads[0].start()
    load_basis(NEXT)
    load_basis(PREV)
    pw_loads[2].start()
    pw_loads[3].start()
    load_basis(OWN)
    small_loads = [
        pltpu.make_async_copy(src, dst, small_sem.at[k])
        for k, (src, dst) in enumerate(
            (
                (occ_hbm, occ_ref), (emp_hbm, emp_ref), (oe_hbm, oe_ref),
                (ee_hbm, ee_ref), (fg_hbm, fg_ref), (fi_hbm, fi_ref),
            )
        )
    ]
    for load in small_loads:
        load.start()

    barrier = pltpu.get_barrier_semaphore()
    for peer in peers:
        pl.semaphore_signal(barrier, inc=1, device_id=peer, device_id_type=MESH)

    def remote(src, dst, s_sem, r_sem, dev):
        return pltpu.make_async_remote_copy(
            src_ref=src, dst_ref=dst, send_sem=s_sem, recv_sem=r_sem, device_id=dev, device_id_type=MESH
        )

    y_sent, c_sent, gap_sent = send_sem.at[0], send_sem.at[1], send_sem.at[2]

    def arrived(dst, sem):
        pltpu.make_async_copy(dst, dst, sem).wait()

    def project(g, d):
        if d == FAR:
            pw_loads[g].wait()
        if g == 1:
            arrived(basis.at[ys[d]], load_sem.at[NG + d])
        part[ys[d], group(g), :] = jnp.dot(
            pw[group(g), :], basis[ys[d]], preferred_element_type=F32
        ).astype(BF16)

    def chunks(g):
        return range(g * GC, (g + 1) * GC)

    def mine(c, d):
        return hs.at[ys[d]] if c == 0 else part.at[ys[d], chunk(c)]

    kept = pl.ds(pl.multiple_of(x_lo * CP, CP), CP)
    given = pl.ds(pl.multiple_of((1 - x_lo) * CP, CP), CP)

    def x_give(d):
        project(0, d)
        remote(part.at[ys[d], given], hx.at[ys[d]], y_sent, h_recv.at[0, d], dev_x).start()

    def x_take(d):
        arrived(hx.at[ys[d]], h_recv.at[0, d])
        hs[ys[d]] = (part[ys[d], kept, :].astype(F32) + hx[ys[d]].astype(F32)).astype(BF16)

    low, high = pl.ds(0, HP), pl.ds(HP, HP)

    def y_far(c):
        remote(mine(c, FAR).at[low], tab.at[c, 0], y_sent, y_recv.at[c, 0], dev_yn).start()
        remote(mine(c, FAR).at[high], tab.at[c, 1], y_sent, y_recv.at[c, 0], dev_yp).start()

    def y_next_half(c):
        remote(mine(c, NEXT).at[high], r12.at[c, 0, high], y_sent, y_recv.at[c, 1], dev_yn).start()

    def y_prev_half(c):
        remote(mine(c, PREV).at[low], r12.at[c, 1, low], y_sent, y_recv.at[c, 1], dev_yp).start()

    def y_second(c):
        arrived(tab.at[c], y_recv.at[c, 0])
        sab[c, 0] = (tab[c, 0].astype(F32) + mine(c, NEXT)[low, :].astype(F32)).astype(BF16)
        remote(sab.at[c, 0], r12.at[c, 0, low], y_sent, y_recv.at[c, 1], dev_yn).start()
        sab[c, 1] = (tab[c, 1].astype(F32) + mine(c, PREV)[high, :].astype(F32)).astype(BF16)
        remote(sab.at[c, 1], r12.at[c, 1, high], y_sent, y_recv.at[c, 1], dev_yp).start()

    def y_total(c):
        arrived(r12.at[c], y_recv.at[c, 1])
        return (mine(c, OWN)[...].astype(F32) + r12[c, 0].astype(F32) + r12[c, 1].astype(F32)).astype(BF16)

    def x_swap(c):
        xs[c] = y_total(c)
        remote(xs.at[c], xr.at[c], y_sent, y_recv.at[c, 2], dev_x).start()

    def group_far(g):
        project(g, FAR)
        for c in chunks(g):
            y_far(c)

    def group_near(g):
        project(g, NEXT)
        for c in chunks(g):
            y_next_half(c)
        project(g, PREV)
        for c in chunks(g):
            y_prev_half(c)

    def group_second(g):
        for c in chunks(g):
            y_second(c)

    def group_swap(g):
        for c in chunks(g):
            x_swap(c)

    def first_far():
        x_take(FAR)
        y_far(0)

    def first_near():
        x_take(NEXT)
        y_next_half(0)
        x_take(PREV)
        y_prev_half(0)

    def x_share(d):
        piece = cf.at[ys[d], kept]
        remote(piece, piece, y_sent, h_recv.at[1, d], dev_x).start()

    def x_shared(d):
        arrived(cf.at[ys[d], given], h_recv.at[1, d])
        to_core(0, d)

    def first_third():
        x_take(OWN)
        cf[ys[OWN], kept, :] = y_total(0)
        piece = cf.at[ys[OWN], kept]
        remote(piece, piece, y_sent, g_recv.at[0, 0], dev_yn).start()
        remote(piece, piece, y_sent, g_recv.at[0, 1], dev_yp).start()
        x_share(OWN)

    def kept_half(h):
        return pl.ds(pl.multiple_of(x_lo * CP + h * HP, HP), HP)

    def first_take():
        arrived(cf.at[ys[PREV], kept], g_recv.at[0, 0])
        x_share(PREV)
        arrived(cf.at[ys[NEXT], kept], g_recv.at[0, 1])
        x_share(NEXT)

    def first_forward():
        piece = cf.at[ys[PREV], kept_half(0)]
        remote(piece, piece, y_sent, g_recv.at[0, 2], dev_yn).start()
        piece = cf.at[ys[NEXT], kept_half(1)]
        remote(piece, piece, y_sent, g_recv.at[0, 2], dev_yp).start()

    def first_last():
        arrived(cf.at[ys[FAR], kept], g_recv.at[0, 2])
        x_share(FAR)

    def to_core(g, d):
        sem = c_recv.at[g] if d == OWN else c_recv.at[NG + d - 1]
        remote(cf.at[ys[d], group(g)], cf.at[ys[d], pl.ds(PL + g * GP, GP)], c_sent, sem, dev_core).start()

    def from_core(d):
        arrived(cf.at[ys[d], pl.ds(PL, PL)], c_recv.at[NG + d - 1])

    def y_third(g):
        for c in chunks(g):
            arrived(xr.at[c], y_recv.at[c, 2])
            cf[ys[OWN], chunk(c), :] = (xs[c].astype(F32) + xr[c].astype(F32)).astype(BF16)
            piece = cf.at[ys[OWN], chunk(c)]
            remote(piece, piece, y_sent, g_recv.at[g, 0], dev_yn).start()
            remote(piece, piece, y_sent, g_recv.at[g, 1], dev_yp).start()
        to_core(g, OWN)

    def y_take(g):
        arrived(cf.at[ys[PREV], group(g)], g_recv.at[g, 0])
        to_core(g, PREV)
        arrived(cf.at[ys[NEXT], group(g)], g_recv.at[g, 1])
        to_core(g, NEXT)

    def y_forward(g):
        piece = cf.at[ys[PREV], group_half(g, 0)]
        remote(piece, piece, y_sent, g_recv.at[g, 2], dev_yn).start()
        piece = cf.at[ys[NEXT], group_half(g, 1)]
        remote(piece, piece, y_sent, g_recv.at[g, 2], dev_yp).start()

    def y_last(g):
        arrived(cf.at[ys[FAR], group(g)], g_recv.at[g, 2])
        to_core(g, FAR)

    def find_gaps():
        for load in small_loads:
            load.wait()

        def occupied(e, value):
            return jnp.where(occ_ref[...] == e, oe_ref[e], value)

        def empty(e, value):
            return jnp.where(emp_ref[...] == e, ee_ref[e], value)

        zero = jnp.zeros((8, 128), F32)
        below = lax.fori_loop(0, 64, occupied, zero, unroll=8)
        above = lax.fori_loop(0, 256, empty, zero, unroll=8)
        gaps[0] = above - below

    def send_gaps():
        remote(gaps.at[0], gaps.at[1], gap_sent, c_recv.at[NG + 3], dev_core).start()

    def find_factors():
        arrived(gaps.at[1], c_recv.at[NG + 3])
        for n in range(NW):
            frequency = fg_ref[fi_ref[core * NW + n]]
            for src in range(2):
                gap = gaps[src]
                below, above = frequency - gap, frequency + gap
                fac[src, n] = (4.0 / PAIRS) * (
                    below / (below * below + broadening_sq) - above / (above * above + broadening_sq)
                )

    def weigh(g, src):
        if src:
            arrived(cf.at[ys[OWN], pl.ds(PL + g * GP, GP)], c_recv.at[g])
        rows = pl.ds(pl.multiple_of(x_lo * ROWS, ROWS), ROWS)
        for r in range(GP // 128):
            first = src * PL + g * GP + r * 128
            block = cf[ys[OWN], pl.ds(first, 128), rows].astype(F32).T

            def one(n, carry):
                row = fac[src, n, pl.ds(g * (GP // 128) + r, 1), :]
                wt[pl.ds(pl.multiple_of(n * ROWS, ROWS), ROWS), pl.ds(first, 128)] = (
                    block * row
                ).astype(BF16)
                return carry

            lax.fori_loop(0, NW, one, 0, unroll=2)

    slot = [ys[d] % 2 for d in range(4)]
    root = [(z % 2) == ys[d] // 2 for d in range(4)]
    here, there = pl.ds(0, ROWS), pl.ds(ROWS, ROWS)

    def cols(t):
        return pl.ds(pl.multiple_of((t // 2) * 128, 128), 128)

    def tiles(d, q):
        val[d, q] = jnp.dot(wt[pl.ds(q * QR, QR), :], cf[ys[d]], preferred_element_type=F32)

        @pl.when(root[d])
        def _():
            zo[d, q, 0] = val[d, q, here, cols(z_far)].astype(BF16)
            remote(zo.at[d, q, 0], zt.at[slot[d], q, 0], c_sent, z_recv.at[d, q], dev_zn).start()
            zo[d, q, 1] = val[d, q, there, cols(z_far)].astype(BF16)
            remote(zo.at[d, q, 1], zt.at[slot[d], q, 1], c_sent, z_recv.at[d, q], dev_zp).start()

        @pl.when(jnp.logical_not(root[d]))
        def _():
            zo[d, q, 0] = val[d, q, there, cols(z_next)].astype(BF16)
            remote(zo.at[d, q, 0], zr.at[slot[d], q, 2], c_sent, z_recv.at[d, q], dev_zn).start()
            zo[d, q, 1] = val[d, q, here, cols(z_prev)].astype(BF16)
            remote(zo.at[d, q, 1], zr.at[slot[d], q, 3], c_sent, z_recv.at[d, q], dev_zp).start()

    def z_second(d, q):
        @pl.when(jnp.logical_not(root[d]))
        def _():
            arrived(zt.at[slot[d], q], z_recv.at[d, q])
            zs[slot[d], q, 0] = (val[d, q, here, cols(z_next)] + zt[slot[d], q, 0].astype(F32)).astype(BF16)
            remote(zs.at[slot[d], q, 0], zr.at[slot[d], q, 0], c_sent, z_recv.at[d, q], dev_zn).start()
            zs[slot[d], q, 1] = (val[d, q, there, cols(z_prev)] + zt[slot[d], q, 1].astype(F32)).astype(BF16)
            remote(zs.at[slot[d], q, 1], zr.at[slot[d], q, 1], c_sent, z_recv.at[d, q], dev_zp).start()

    ours = pl.ds(pl.multiple_of(core * 64, 64), 64)
    theirs = pl.ds(pl.multiple_of((1 - core) * 64, 64), 64)

    def z_third(d, q):
        @pl.when(root[d])
        def _():
            arrived(zr.at[slot[d], q], z_recv.at[d, q])

            def total(rows, first, second):
                return (
                    val[d, q, rows, cols(z)]
                    + zr[slot[d], q, first].astype(F32)
                    + zr[slot[d], q, second].astype(F32)
                ).T

            @pl.when(slot[d] == x_hi)
            def _():
                fin[2 * q] = total(here, 0, 3)
                fin[2 * q + 1] = total(there, 2, 1)
                remote(
                    fin.at[pl.ds(2 * q, 2), theirs, :], finr.at[pl.ds(2 * q, 2)], c_sent, x_recv.at[q, 2], dev_core
                ).start()

            @pl.when(slot[d] != x_hi)
            def _():
                zxs[q, 0] = total(here, 0, 3).astype(BF16)
                zxs[q, 1] = total(there, 2, 1).astype(BF16)
                remote(zxs.at[q, :, ours, :], zxr.at[q, 0], c_sent, x_recv.at[q, 0], dev_xh).start()
                remote(zxs.at[q, :, theirs, :], zxr.at[q, 1], c_sent, x_recv.at[q, 1], dev_xhc).start()

    def finish(q):
        arrived(zxr.at[q, 0], x_recv.at[q, 0])
        out_ref[pl.ds(core * NW + 2 * q, 2)] = fin[pl.ds(2 * q, 2), ours, :] + zxr[q, 0].astype(F32)
        arrived(finr.at[pl.ds(2 * q, 2)], x_recv.at[q, 2])
        arrived(zxr.at[q, 1], x_recv.at[q, 1])
        out_ref[pl.ds((1 - core) * NW + 2 * q, 2)] = finr[pl.ds(2 * q, 2)] + zxr[q, 1].astype(F32)

    project(1, FAR)
    pl.semaphore_wait(barrier, len(peers))
    y_far(2)
    y_far(3)
    x_give(FAR)
    group_far(2)
    group_near(1)
    x_give(NEXT)
    group_second(1)
    x_give(PREV)
    group_far(3)
    first_far()
    group_near(2)
    group_second(2)
    project(1, OWN)
    first_near()
    group_swap(1)
    x_give(OWN)
    group_near(3)
    y_second(0)
    group_second(3)
    project(2, OWN)
    find_gaps()
    send_gaps()
    group_swap(2)
    project(3, OWN)
    first_third()
    y_third(1)
    group_swap(3)
    find_factors()
    y_third(2)
    weigh(1, 0)
    x_shared(OWN)
    weigh(1, 1)
    weigh(2, 0)
    weigh(0, 0)
    weigh(2, 1)
    y_third(3)
    weigh(3, 0)
    weigh(0, 1)
    first_take()
    first_forward()
    weigh(3, 1)
    tiles(OWN, 0)
    tiles(OWN, 1)
    y_take(1)
    tiles(OWN, 2)
    tiles(OWN, 3)
    x_shared(PREV)
    x_shared(NEXT)
    y_take(2)
    y_forward(1)
    y_take(3)
    y_forward(2)
    y_forward(3)
    z_second(OWN, 0)
    z_second(OWN, 1)
    from_core(NEXT)
    for q in range(NQ):
        tiles(NEXT, q)
        if q < 2:
            z_second(OWN, q + 2)
    from_core(PREV)
    first_last()
    tiles(PREV, 0)
    z_third(OWN, 0)
    z_second(NEXT, 0)
    y_last(1)
    tiles(PREV, 1)
    z_third(OWN, 1)
    z_second(NEXT, 1)
    y_last(2)
    tiles(PREV, 2)
    z_third(OWN, 2)
    z_second(NEXT, 2)
    x_shared(FAR)
    y_last(3)
    tiles(PREV, 3)
    z_third(OWN, 3)
    z_second(NEXT, 3)
    from_core(FAR)
    for q in range(NQ):
        z_second(PREV, q)
        tiles(FAR, q)
    for q in range(NQ):
        z_third(NEXT, q)
    for q in range(NQ):
        z_second(FAR, q)
        z_third(PREV, q)
    for q in range(NQ):
        z_third(FAR, q)
    for q in range(NQ):
        finish(q)
    arrived(pw.at[pl.ds(0, 896)], y_sent)
    arrived(pw, c_sent)
    arrived(gaps.at[0], gap_sent)


def on_device(pair_waves, subspace_basis, occ_band, empty_band, occ_energy, empty_energy, freq_grid, freq_index):
    vmem = pl.BlockSpec(memory_space=pltpu.VMEM)
    hbm = pl.BlockSpec(memory_space=pltpu.HBM)
    dma = pltpu.SemaphoreType.DMA
    out = pl.pallas_call(
        kernel,
        out_shape=jax.ShapeDtypeStruct((NFREQ, 64, ROWS), F32),
        in_specs=[hbm] * 8,
        out_specs=vmem,
        scratch_shapes=[
            pltpu.VMEM((8, 128), jnp.int32),
            pltpu.VMEM((8, 128), jnp.int32),
            pltpu.SMEM((64,), F32),
            pltpu.SMEM((256,), F32),
            pltpu.SMEM((NFREQ,), F32),
            pltpu.SMEM((NFREQ,), jnp.int32),
            pltpu.VMEM((PL, PWL), BF16),
            pltpu.VMEM((4, PWL, BC), BF16),
            pltpu.VMEM((4, PL, BC), BF16),
            pltpu.VMEM((4, 2 * PL, BC), BF16),
            pltpu.VMEM((NW * ROWS, 2 * PL), BF16),
            pltpu.VMEM((2, 8, 128), F32),
            pltpu.VMEM((2, NW, 8, 128), F32),
            pltpu.VMEM((4, CP, BC), BF16),
            pltpu.VMEM((4, CP, BC), BF16),
            pltpu.VMEM((NC, 2, HP, BC), BF16),
            pltpu.VMEM((NC, 2, HP, BC), BF16),
            pltpu.VMEM((NC, 2, CP, BC), BF16),
            pltpu.VMEM((NC, CP, BC), BF16),
            pltpu.VMEM((NC, CP, BC), BF16),
            pltpu.VMEM((4, NQ, QR, BC), F32),
            pltpu.VMEM((4, NQ, 2, ROWS, ROWS), BF16),
            pltpu.VMEM((2, NQ, 2, ROWS, ROWS), BF16),
            pltpu.VMEM((2, NQ, 2, ROWS, ROWS), BF16),
            pltpu.VMEM((2, NQ, 4, ROWS, ROWS), BF16),
            pltpu.VMEM((NQ, 2, ROWS, ROWS), BF16),
            pltpu.VMEM((NQ, 2, 2, 64, ROWS), BF16),
            pltpu.VMEM((NW, ROWS, ROWS), F32),
            pltpu.VMEM((NW, 64, ROWS), F32),
            dma((NG + 4,)),
            dma((6,)),
            dma((3,)),
            dma((NC, 3)),
            dma((NG, 3)),
            dma((2, 4)),
            dma((4, NQ)),
            dma((NQ, 3)),
            dma((NG + 4,)),
        ],
        compiler_params=pltpu.CompilerParams(collective_id=0, has_side_effects=True, vmem_limit_bytes=48 << 20),
        cost_estimate=pl.CostEstimate(flops=9 << 30, bytes_accessed=9 << 20, transcendentals=0),
    )(
        *(
            pltpu.with_memory_space_constraint(array, pltpu.HBM)
            for array in (
                occ_band.reshape(8, 128), empty_band.reshape(8, 128), pair_waves, subspace_basis,
                occ_energy, empty_energy, freq_grid, freq_index,
            )
        )
    )
    return jnp.swapaxes(out, 1, 2)


def solution(mesh):
    return jax.shard_map(
        on_device,
        mesh=mesh,
        in_specs=(P("pair", "pw"), P("pw", None), P("pair"), P("pair"), P(), P(), P(), P()),
        out_specs=P(None, "pw", "pair"),
        check_vma=False,
    )
```

```python
import jax
import jax.numpy as jnp
from jax import lax
from jax.experimental import pallas as pl
from jax.experimental.pallas import tpu as pltpu
from jax.sharding import PartitionSpec as P

F32, BF16 = jnp.float32, jnp.bfloat16
MESH = pl.DeviceIdType.MESH
broadening_sq = 0.0025

PAIRS = 16384
NFREQ = 16
NW = 8
NB = 1024
PL = 1024
PWL = 2048
ROWS = 128
BC = 256
NC = 8
CP = PL // NC
HP = CP // 2
NG = 4
GP = PL // NG
GC = NC // NG
NQ = 4
QR = NW * ROWS // NQ
OWN, NEXT, FAR, PREV = range(4)
SECOND, THIRD = NEXT, PREV


def kernel(
    occ_hbm, emp_hbm, pw_hbm, basis_hbm, oe_hbm, ee_hbm, fg_hbm, fi_hbm, out_ref,
    occ_ref, emp_ref, oe_ref, ee_ref, fg_ref, fi_ref,
    pw, basis, part, cf, wt, gaps, fac,
    hx, hs, tab, sab, r12, xs, xr,
    val, zo, zs, zt, zr, zxs, zxr, fin, finr,
    load_sem, small_sem, send_sem, y_recv, g_recv, h_recv, z_recv, x_recv, c_recv,
):
    me_pw, me_pair = lax.axis_index("pw"), lax.axis_index("pair")
    x_lo, y = me_pw // 4, me_pw % 4
    z, x_hi, core = me_pair // 4, (me_pair // 2) % 2, me_pair % 2
    ys = [(y + d) % 4 for d in range(4)]
    z_next, z_prev, z_far = (z + 1) % 4, (z + 3) % 4, (z + 2) % 4

    def along_y(t):
        return (x_lo * 4 + t, me_pair)

    def along_z(t):
        return (me_pw, t * 4 + me_pair % 4)

    dev_yn, dev_yp = along_y(ys[NEXT]), along_y(ys[PREV])
    dev_zn, dev_zp = along_z(z_next), along_z(z_prev)
    dev_x = ((me_pw + 4) % 8, me_pair)
    dev_xh = (me_pw, z * 4 + (me_pair + 2) % 4)
    dev_xhc = (me_pw, z * 4 + ((me_pair // 2) * 2 + 3 - core) % 4)
    dev_core = (me_pw, (me_pair // 2) * 2 + 1 - core)
    peers = (dev_yn, dev_yp, dev_zn, dev_zp, dev_x, dev_xh, dev_xhc, dev_core)

    def chunk(c):
        return pl.ds(c * CP, CP)

    def half(c, h):
        return pl.ds(c * CP + h * HP, HP)

    def group(g):
        return pl.ds(g * GP, GP)

    def group_half(g, h):
        return pl.ds(g * GP + h * (GP // 2), GP // 2)

    pw_loads = [pltpu.make_async_copy(pw_hbm.at[group(g)], pw.at[group(g)], load_sem.at[g]) for g in range(NG)]
    def load_basis(d):
        for l in range(2):
            pltpu.make_async_copy(
                basis_hbm.at[:, pl.ds(pl.multiple_of(l * 512 + ys[d] * 128, 128), 128)],
                basis.at[ys[d], :, pl.ds(l * 128, 128)],
                load_sem.at[NG + d],
            ).start()

    load_basis(FAR)
    pw_loads[1].start()
    pw_loads[0].start()
    load_basis(NEXT)
    load_basis(PREV)
    pw_loads[2].start()
    pw_loads[3].start()
    load_basis(OWN)
    small_loads = [
        pltpu.make_async_copy(src, dst, small_sem.at[k])
        for k, (src, dst) in enumerate(
            (
                (occ_hbm, occ_ref), (emp_hbm, emp_ref), (oe_hbm, oe_ref),
                (ee_hbm, ee_ref), (fg_hbm, fg_ref), (fi_hbm, fi_ref),
            )
        )
    ]
    for load in small_loads:
        load.start()

    barrier = pltpu.get_barrier_semaphore()
    for peer in peers:
        pl.semaphore_signal(barrier, inc=1, device_id=peer, device_id_type=MESH)

    def remote(src, dst, s_sem, r_sem, dev):
        return pltpu.make_async_remote_copy(
            src_ref=src, dst_ref=dst, send_sem=s_sem, recv_sem=r_sem, device_id=dev, device_id_type=MESH
        )

    y_sent, c_sent, gap_sent = send_sem.at[0], send_sem.at[1], send_sem.at[2]

    def arrived(dst, sem):
        pltpu.make_async_copy(dst, dst, sem).wait()

    def project(g, d):
        if d == FAR:
            pw_loads[g].wait()
        if g == 1:
            arrived(basis.at[ys[d]], load_sem.at[NG + d])
        part[ys[d], group(g), :] = jnp.dot(
            pw[group(g), :], basis[ys[d]], preferred_element_type=F32
        ).astype(BF16)

    def chunks(g):
        return range(g * GC, (g + 1) * GC)

    def mine(c, d):
        return hs.at[ys[d]] if c == 0 else part.at[ys[d], chunk(c)]

    kept = pl.ds(pl.multiple_of(x_lo * CP, CP), CP)
    given = pl.ds(pl.multiple_of((1 - x_lo) * CP, CP), CP)

    def x_give(d):
        project(0, d)
        remote(part.at[ys[d], given], hx.at[ys[d]], y_sent, h_recv.at[0, d], dev_x).start()

    def x_take(d):
        arrived(hx.at[ys[d]], h_recv.at[0, d])
        hs[ys[d]] = (part[ys[d], kept, :].astype(F32) + hx[ys[d]].astype(F32)).astype(BF16)

    low, high = pl.ds(0, HP), pl.ds(HP, HP)

    def y_far(c):
        remote(mine(c, FAR).at[low], tab.at[c, 0], y_sent, y_recv.at[c, 0], dev_yn).start()
        remote(mine(c, FAR).at[high], tab.at[c, 1], y_sent, y_recv.at[c, 0], dev_yp).start()

    def y_next_half(c):
        remote(mine(c, NEXT).at[high], r12.at[c, 0, high], y_sent, y_recv.at[c, 1], dev_yn).start()

    def y_prev_half(c):
        remote(mine(c, PREV).at[low], r12.at[c, 1, low], y_sent, y_recv.at[c, 1], dev_yp).start()

    def y_second(c):
        arrived(tab.at[c], y_recv.at[c, 0])
        sab[c, 0] = (tab[c, 0].astype(F32) + mine(c, NEXT)[low, :].astype(F32)).astype(BF16)
        remote(sab.at[c, 0], r12.at[c, 0, low], y_sent, y_recv.at[c, 1], dev_yn).start()
        sab[c, 1] = (tab[c, 1].astype(F32) + mine(c, PREV)[high, :].astype(F32)).astype(BF16)
        remote(sab.at[c, 1], r12.at[c, 1, high], y_sent, y_recv.at[c, 1], dev_yp).start()

    def y_total(c):
        arrived(r12.at[c], y_recv.at[c, 1])
        return (mine(c, OWN)[...].astype(F32) + r12[c, 0].astype(F32) + r12[c, 1].astype(F32)).astype(BF16)

    def x_swap(c):
        xs[c] = y_total(c)
        remote(xs.at[c], xr.at[c], y_sent, y_recv.at[c, 2], dev_x).start()

    def group_far(g):
        project(g, FAR)
        for c in chunks(g):
            y_far(c)

    def group_near(g):
        project(g, NEXT)
        for c in chunks(g):
            y_next_half(c)
        project(g, PREV)
        for c in chunks(g):
            y_prev_half(c)

    def group_second(g):
        for c in chunks(g):
            y_second(c)

    def group_swap(g):
        for c in chunks(g):
            x_swap(c)

    def first_far():
        x_take(FAR)
        y_far(0)

    def first_near():
        x_take(NEXT)
        y_next_half(0)
        x_take(PREV)
        y_prev_half(0)

    def x_share(d):
        piece = cf.at[ys[d], kept]
        remote(piece, piece, y_sent, h_recv.at[1, d], dev_x).start()

    def x_shared(d):
        arrived(cf.at[ys[d], given], h_recv.at[1, d])
        to_core(0, d)

    def first_third():
        x_take(OWN)
        cf[ys[OWN], kept, :] = y_total(0)
        piece = cf.at[ys[OWN], kept]
        remote(piece, piece, y_sent, g_recv.at[0, 0], dev_yn).start()
        remote(piece, piece, y_sent, g_recv.at[0, 1], dev_yp).start()
        x_share(OWN)

    def kept_half(h):
        return pl.ds(pl.multiple_of(x_lo * CP + h * HP, HP), HP)

    def first_take():
        arrived(cf.at[ys[PREV], kept], g_recv.at[0, 0])
        x_share(PREV)
        arrived(cf.at[ys[NEXT], kept], g_recv.at[0, 1])
        x_share(NEXT)

    def first_forward():
        piece = cf.at[ys[PREV], kept_half(0)]
        remote(piece, piece, y_sent, g_recv.at[0, 2], dev_yn).start()
        piece = cf.at[ys[NEXT], kept_half(1)]
        remote(piece, piece, y_sent, g_recv.at[0, 2], dev_yp).start()

    def first_last():
        arrived(cf.at[ys[FAR], kept], g_recv.at[0, 2])
        x_share(FAR)

    def to_core(g, d):
        sem = c_recv.at[g] if d == OWN else c_recv.at[NG + d - 1]
        remote(cf.at[ys[d], group(g)], cf.at[ys[d], pl.ds(PL + g * GP, GP)], c_sent, sem, dev_core).start()

    def y_third(g):
        for c in chunks(g):
            arrived(xr.at[c], y_recv.at[c, 2])
            cf[ys[OWN], chunk(c), :] = (xs[c].astype(F32) + xr[c].astype(F32)).astype(BF16)
            piece = cf.at[ys[OWN], chunk(c)]
            remote(piece, piece, y_sent, g_recv.at[g, 0], dev_yn).start()
            remote(piece, piece, y_sent, g_recv.at[g, 1], dev_yp).start()
        to_core(g, OWN)

    def y_take(g):
        arrived(cf.at[ys[PREV], group(g)], g_recv.at[g, 0])
        to_core(g, PREV)
        arrived(cf.at[ys[NEXT], group(g)], g_recv.at[g, 1])
        to_core(g, NEXT)

    def y_forward(g):
        piece = cf.at[ys[PREV], group_half(g, 0)]
        remote(piece, piece, y_sent, g_recv.at[g, 2], dev_yn).start()
        piece = cf.at[ys[NEXT], group_half(g, 1)]
        remote(piece, piece, y_sent, g_recv.at[g, 2], dev_yp).start()

    def y_last(g):
        arrived(cf.at[ys[FAR], group(g)], g_recv.at[g, 2])
        to_core(g, FAR)

    def find_gaps():
        for load in small_loads:
            load.wait()

        def occupied(e, value):
            return jnp.where(occ_ref[...] == e, oe_ref[e], value)

        def empty(e, value):
            return jnp.where(emp_ref[...] == e, ee_ref[e], value)

        zero = jnp.zeros((8, 128), F32)
        below = lax.fori_loop(0, 64, occupied, zero, unroll=8)
        above = lax.fori_loop(0, 256, empty, zero, unroll=8)
        gaps[0] = above - below

    def send_gaps():
        remote(gaps.at[0], gaps.at[1], gap_sent, c_recv.at[NG + 3], dev_core).start()

    def find_factors():
        arrived(gaps.at[1], c_recv.at[NG + 3])
        for n in range(NW):
            frequency = fg_ref[fi_ref[core * NW + n]]
            for src in range(2):
                gap = gaps[src]
                below, above = frequency - gap, frequency + gap
                fac[src, n] = (4.0 / PAIRS) * (
                    below / (below * below + broadening_sq) - above / (above * above + broadening_sq)
                )

    def weigh(g, src):
        if src:
            arrived(cf.at[ys[OWN], pl.ds(PL + g * GP, GP)], c_recv.at[g])
        rows = pl.ds(pl.multiple_of(x_lo * ROWS, ROWS), ROWS)
        for r in range(GP // 128):
            first = src * PL + g * GP + r * 128
            block = cf[ys[OWN], pl.ds(first, 128), rows].astype(F32).T

            def one(n, carry):
                row = fac[src, n, pl.ds(g * (GP // 128) + r, 1), :]
                wt[pl.ds(pl.multiple_of(n * ROWS, ROWS), ROWS), pl.ds(first, 128)] = (
                    block * row
                ).astype(BF16)
                return carry

            lax.fori_loop(0, NW, one, 0, unroll=2)

    turn = [OWN, 3 - 2 * (y % 2), FAR, 1 + 2 * (y % 2)]
    yt = [ys[OWN], (y + 3 - 2 * (y % 2)) % 4, ys[FAR], (y + 1 + 2 * (y % 2)) % 4]
    slot = [yt[d] % 2 for d in range(4)]
    root = [(z % 2) == yt[d] // 2 for d in range(4)]

    def whole(d):
        arrived(cf.at[yt[d], pl.ds(PL, PL)], c_recv.at[NG + turn[d] - 1])

    here, there = pl.ds(0, ROWS), pl.ds(ROWS, ROWS)

    def cols(t):
        return pl.ds(pl.multiple_of((t // 2) * 128, 128), 128)

    def tiles(d, q):
        val[d, q] = jnp.dot(wt[pl.ds(q * QR, QR), :], cf[yt[d]], preferred_element_type=F32)

        @pl.when(root[d])
        def _():
            zo[d, q, 0] = val[d, q, here, cols(z_far)].astype(BF16)
            remote(zo.at[d, q, 0], zt.at[slot[d], q, 0], c_sent, z_recv.at[d, q], dev_zn).start()
            zo[d, q, 1] = val[d, q, there, cols(z_far)].astype(BF16)
            remote(zo.at[d, q, 1], zt.at[slot[d], q, 1], c_sent, z_recv.at[d, q], dev_zp).start()

        @pl.when(jnp.logical_not(root[d]))
        def _():
            zo[d, q, 0] = val[d, q, there, cols(z_next)].astype(BF16)
            remote(zo.at[d, q, 0], zr.at[slot[d], q, 2], c_sent, z_recv.at[d, q], dev_zn).start()
            zo[d, q, 1] = val[d, q, here, cols(z_prev)].astype(BF16)
            remote(zo.at[d, q, 1], zr.at[slot[d], q, 3], c_sent, z_recv.at[d, q], dev_zp).start()

    def z_second(d, q):
        @pl.when(jnp.logical_not(root[d]))
        def _():
            arrived(zt.at[slot[d], q], z_recv.at[d, q])
            zs[slot[d], q, 0] = (val[d, q, here, cols(z_next)] + zt[slot[d], q, 0].astype(F32)).astype(BF16)
            remote(zs.at[slot[d], q, 0], zr.at[slot[d], q, 0], c_sent, z_recv.at[d, q], dev_zn).start()
            zs[slot[d], q, 1] = (val[d, q, there, cols(z_prev)] + zt[slot[d], q, 1].astype(F32)).astype(BF16)
            remote(zs.at[slot[d], q, 1], zr.at[slot[d], q, 1], c_sent, z_recv.at[d, q], dev_zp).start()

    ours = pl.ds(pl.multiple_of(core * 64, 64), 64)
    theirs = pl.ds(pl.multiple_of((1 - core) * 64, 64), 64)

    def z_third(d, q):
        @pl.when(root[d])
        def _():
            arrived(zr.at[slot[d], q], z_recv.at[d, q])

            def total(rows, first, second):
                return (
                    val[d, q, rows, cols(z)]
                    + zr[slot[d], q, first].astype(F32)
                    + zr[slot[d], q, second].astype(F32)
                ).T

            @pl.when(slot[d] == x_hi)
            def _():
                fin[2 * q] = total(here, 0, 3)
                fin[2 * q + 1] = total(there, 2, 1)
                remote(
                    fin.at[pl.ds(2 * q, 2), theirs, :], finr.at[pl.ds(2 * q, 2)], c_sent, x_recv.at[q, 2], dev_core
                ).start()

            @pl.when(slot[d] != x_hi)
            def _():
                zxs[q, 0] = total(here, 0, 3).astype(BF16)
                zxs[q, 1] = total(there, 2, 1).astype(BF16)
                remote(zxs.at[q, :, ours, :], zxr.at[q, 0], c_sent, x_recv.at[q, 0], dev_xh).start()
                remote(zxs.at[q, :, theirs, :], zxr.at[q, 1], c_sent, x_recv.at[q, 1], dev_xhc).start()

    def finish(q):
        arrived(zxr.at[q, 0], x_recv.at[q, 0])
        out_ref[pl.ds(core * NW + 2 * q, 2)] = fin[pl.ds(2 * q, 2), ours, :] + zxr[q, 0].astype(F32)
        arrived(finr.at[pl.ds(2 * q, 2)], x_recv.at[q, 2])
        arrived(zxr.at[q, 1], x_recv.at[q, 1])
        out_ref[pl.ds((1 - core) * NW + 2 * q, 2)] = finr[pl.ds(2 * q, 2)] + zxr[q, 1].astype(F32)

    project(1, FAR)
    pl.semaphore_wait(barrier, len(peers))
    y_far(2)
    y_far(3)
    x_give(FAR)
    group_far(2)
    group_near(1)
    x_give(NEXT)
    group_second(1)
    x_give(PREV)
    group_far(3)
    first_far()
    group_near(2)
    group_second(2)
    project(1, OWN)
    first_near()
    group_swap(1)
    x_give(OWN)
    group_near(3)
    y_second(0)
    group_second(3)
    project(2, OWN)
    find_gaps()
    send_gaps()
    y_third(1)
    group_swap(2)
    project(3, OWN)
    first_third()
    group_swap(3)
    find_factors()
    y_third(2)
    weigh(1, 0)
    x_shared(OWN)
    weigh(1, 1)
    weigh(2, 0)
    weigh(0, 0)
    weigh(2, 1)
    y_third(3)
    weigh(3, 0)
    weigh(0, 1)
    first_take()
    first_forward()
    weigh(3, 1)
    tiles(OWN, 0)
    tiles(OWN, 1)
    y_take(1)
    tiles(OWN, 2)
    tiles(OWN, 3)
    x_shared(PREV)
    x_shared(NEXT)
    y_take(2)
    y_forward(1)
    y_take(3)
    y_forward(2)
    y_forward(3)
    z_second(OWN, 0)
    z_second(OWN, 1)
    whole(SECOND)
    tiles(SECOND, 0)
    z_second(OWN, 2)
    tiles(SECOND, 1)
    z_second(OWN, 3)
    tiles(SECOND, 2)
    tiles(SECOND, 3)
    first_last()
    whole(THIRD)
    tiles(THIRD, 0)
    y_last(1)
    z_second(SECOND, 0)
    tiles(THIRD, 1)
    z_second(SECOND, 1)
    y_last(2)
    tiles(THIRD, 2)
    y_last(3)
    tiles(THIRD, 3)
    x_shared(FAR)
    z_second(SECOND, 2)
    z_second(SECOND, 3)
    z_third(OWN, 0)
    z_third(OWN, 1)
    z_second(THIRD, 0)
    whole(FAR)
    tiles(FAR, 0)
    tiles(FAR, 1)
    z_second(THIRD, 1)
    tiles(FAR, 2)
    tiles(FAR, 3)
    z_second(THIRD, 2)
    z_second(THIRD, 3)
    for q in range(NQ):
        z_second(FAR, q)
    z_third(OWN, 2)
    z_third(OWN, 3)
    for q in range(NQ):
        z_third(SECOND, q)
    for q in range(NQ):
        z_third(THIRD, q)
    for q in range(NQ):
        z_third(FAR, q)
    for q in range(NQ):
        finish(q)
    arrived(pw.at[pl.ds(0, 896)], y_sent)
    arrived(pw, c_sent)
    arrived(gaps.at[0], gap_sent)


def on_device(pair_waves, subspace_basis, occ_band, empty_band, occ_energy, empty_energy, freq_grid, freq_index):
    vmem = pl.BlockSpec(memory_space=pltpu.VMEM)
    hbm = pl.BlockSpec(memory_space=pltpu.HBM)
    dma = pltpu.SemaphoreType.DMA
    out = pl.pallas_call(
        kernel,
        out_shape=jax.ShapeDtypeStruct((NFREQ, 64, ROWS), F32),
        in_specs=[hbm] * 8,
        out_specs=vmem,
        scratch_shapes=[
            pltpu.VMEM((8, 128), jnp.int32),
            pltpu.VMEM((8, 128), jnp.int32),
            pltpu.SMEM((64,), F32),
            pltpu.SMEM((256,), F32),
            pltpu.SMEM((NFREQ,), F32),
            pltpu.SMEM((NFREQ,), jnp.int32),
            pltpu.VMEM((PL, PWL), BF16),
            pltpu.VMEM((4, PWL, BC), BF16),
            pltpu.VMEM((4, PL, BC), BF16),
            pltpu.VMEM((4, 2 * PL, BC), BF16),
            pltpu.VMEM((NW * ROWS, 2 * PL), BF16),
            pltpu.VMEM((2, 8, 128), F32),
            pltpu.VMEM((2, NW, 8, 128), F32),
            pltpu.VMEM((4, CP, BC), BF16),
            pltpu.VMEM((4, CP, BC), BF16),
            pltpu.VMEM((NC, 2, HP, BC), BF16),
            pltpu.VMEM((NC, 2, HP, BC), BF16),
            pltpu.VMEM((NC, 2, CP, BC), BF16),
            pltpu.VMEM((NC, CP, BC), BF16),
            pltpu.VMEM((NC, CP, BC), BF16),
            pltpu.VMEM((4, NQ, QR, BC), F32),
            pltpu.VMEM((4, NQ, 2, ROWS, ROWS), BF16),
            pltpu.VMEM((2, NQ, 2, ROWS, ROWS), BF16),
            pltpu.VMEM((2, NQ, 2, ROWS, ROWS), BF16),
            pltpu.VMEM((2, NQ, 4, ROWS, ROWS), BF16),
            pltpu.VMEM((NQ, 2, ROWS, ROWS), BF16),
            pltpu.VMEM((NQ, 2, 2, 64, ROWS), BF16),
            pltpu.VMEM((NW, ROWS, ROWS), F32),
            pltpu.VMEM((NW, 64, ROWS), F32),
            dma((NG + 4,)),
            dma((6,)),
            dma((3,)),
            dma((NC, 3)),
            dma((NG, 3)),
            dma((2, 4)),
            dma((4, NQ)),
            dma((NQ, 3)),
            dma((NG + 4,)),
        ],
        compiler_params=pltpu.CompilerParams(collective_id=0, has_side_effects=True, vmem_limit_bytes=48 << 20),
        cost_estimate=pl.CostEstimate(flops=9 << 30, bytes_accessed=9 << 20, transcendentals=0),
    )(
        *(
            pltpu.with_memory_space_constraint(array, pltpu.HBM)
            for array in (
                occ_band.reshape(8, 128), empty_band.reshape(8, 128), pair_waves, subspace_basis,
                occ_energy, empty_energy, freq_grid, freq_index,
            )
        )
    )
    return jnp.swapaxes(out, 1, 2)


def solution(mesh):
    return jax.shard_map(
        on_device,
        mesh=mesh,
        in_specs=(P("pair", "pw"), P("pw", None), P("pair"), P("pair"), P(), P(), P(), P()),
        out_specs=P(None, "pw", "pair"),
        check_vma=False,
    )
```

```python
import jax
import jax.numpy as jnp
from jax import lax
from jax.experimental import pallas as pl
from jax.experimental.pallas import tpu as pltpu
from jax.sharding import PartitionSpec as P

F32, BF16 = jnp.float32, jnp.bfloat16
MESH = pl.DeviceIdType.MESH
broadening_sq = 0.0025

PAIRS = 16384
NFREQ = 16
NW = 8
NB = 1024
PL = 1024
PWL = 2048
ROWS = 128
BC = 256
NC = 8
CP = PL // NC
HP = CP // 2
NG = 4
GP = PL // NG
GC = NC // NG
NQ = 4
QR = NW * ROWS // NQ
OWN, NEXT, FAR, PREV = range(4)
SECOND, THIRD = NEXT, PREV


def kernel(
    occ_hbm, emp_hbm, pw_hbm, basis_hbm, oe_hbm, ee_hbm, fg_hbm, fi_hbm, out_ref,
    occ_ref, emp_ref, oe_ref, ee_ref, fg_ref, fi_ref,
    pw, basis, part, cf, wt, gaps, fac,
    hx, hs, tab, sab, r12, xs, xr,
    val, zo, zs, zt, zr, zxs, zxr, fin, finr,
    load_sem, small_sem, send_sem, y_recv, g_recv, h_recv, z_recv, x_recv, c_recv,
):
    me_pw, me_pair = lax.axis_index("pw"), lax.axis_index("pair")
    x_lo, y = me_pw // 4, me_pw % 4
    z, x_hi, core = me_pair // 4, (me_pair // 2) % 2, me_pair % 2
    ys = [(y + d) % 4 for d in range(4)]
    z_next, z_prev, z_far = (z + 1) % 4, (z + 3) % 4, (z + 2) % 4

    def along_y(t):
        return (x_lo * 4 + t, me_pair)

    def along_z(t):
        return (me_pw, t * 4 + me_pair % 4)

    dev_yn, dev_yp = along_y(ys[NEXT]), along_y(ys[PREV])
    dev_zn, dev_zp = along_z(z_next), along_z(z_prev)
    dev_x = ((me_pw + 4) % 8, me_pair)
    dev_xh = (me_pw, z * 4 + (me_pair + 2) % 4)
    dev_xhc = (me_pw, z * 4 + ((me_pair // 2) * 2 + 3 - core) % 4)
    dev_core = (me_pw, (me_pair // 2) * 2 + 1 - core)
    peers = (dev_yn, dev_yp, dev_zn, dev_zp, dev_x, dev_xh, dev_xhc, dev_core)

    def chunk(c):
        return pl.ds(c * CP, CP)

    def half(c, h):
        return pl.ds(c * CP + h * HP, HP)

    def group(g):
        return pl.ds(g * GP, GP)

    def group_half(g, h):
        return pl.ds(g * GP + h * (GP // 2), GP // 2)

    pw_loads = [pltpu.make_async_copy(pw_hbm.at[group(g)], pw.at[group(g)], load_sem.at[g]) for g in range(NG)]
    def load_basis(d):
        for l in range(2):
            pltpu.make_async_copy(
                basis_hbm.at[:, pl.ds(pl.multiple_of(l * 512 + ys[d] * 128, 128), 128)],
                basis.at[ys[d], :, pl.ds(l * 128, 128)],
                load_sem.at[NG + d],
            ).start()

    load_basis(FAR)
    pw_loads[1].start()
    pw_loads[0].start()
    load_basis(NEXT)
    load_basis(PREV)
    pw_loads[2].start()
    pw_loads[3].start()
    load_basis(OWN)
    small_loads = [
        pltpu.make_async_copy(src, dst, small_sem.at[k])
        for k, (src, dst) in enumerate(
            (
                (occ_hbm, occ_ref), (emp_hbm, emp_ref), (oe_hbm, oe_ref),
                (ee_hbm, ee_ref), (fg_hbm, fg_ref), (fi_hbm, fi_ref),
            )
        )
    ]
    for load in small_loads:
        load.start()

    barrier = pltpu.get_barrier_semaphore()
    for peer in peers:
        pl.semaphore_signal(barrier, inc=1, device_id=peer, device_id_type=MESH)

    def remote(src, dst, s_sem, r_sem, dev):
        return pltpu.make_async_remote_copy(
            src_ref=src, dst_ref=dst, send_sem=s_sem, recv_sem=r_sem, device_id=dev, device_id_type=MESH
        )

    y_sent, c_sent, gap_sent = send_sem.at[0], send_sem.at[1], send_sem.at[2]

    def arrived(dst, sem):
        pltpu.make_async_copy(dst, dst, sem).wait()

    def project(g, d):
        if d == FAR:
            pw_loads[g].wait()
        if g == 1:
            arrived(basis.at[ys[d]], load_sem.at[NG + d])
        part[ys[d], group(g), :] = jnp.dot(
            pw[group(g), :], basis[ys[d]], preferred_element_type=F32
        ).astype(BF16)

    def first_loads():
        pw_loads[1].wait()
        arrived(basis.at[ys[FAR]], load_sem.at[NG + FAR])

    def project_chunk(c):
        part[ys[FAR], chunk(c), :] = jnp.dot(
            pw[chunk(c), :], basis[ys[FAR]], preferred_element_type=F32
        ).astype(BF16)

    def chunks(g):
        return range(g * GC, (g + 1) * GC)

    def mine(c, d):
        return hs.at[ys[d]] if c == 0 else part.at[ys[d], chunk(c)]

    kept = pl.ds(pl.multiple_of(x_lo * CP, CP), CP)
    given = pl.ds(pl.multiple_of((1 - x_lo) * CP, CP), CP)

    def x_give(d):
        project(0, d)
        remote(part.at[ys[d], given], hx.at[ys[d]], y_sent, h_recv.at[0, d], dev_x).start()

    def x_take(d):
        arrived(hx.at[ys[d]], h_recv.at[0, d])
        hs[ys[d]] = (part[ys[d], kept, :].astype(F32) + hx[ys[d]].astype(F32)).astype(BF16)

    low, high = pl.ds(0, HP), pl.ds(HP, HP)

    def y_far(c):
        remote(mine(c, FAR).at[low], tab.at[c, 0], y_sent, y_recv.at[c, 0], dev_yn).start()
        remote(mine(c, FAR).at[high], tab.at[c, 1], y_sent, y_recv.at[c, 0], dev_yp).start()

    def y_next_half(c):
        remote(mine(c, NEXT).at[high], r12.at[c, 0, high], y_sent, y_recv.at[c, 1], dev_yn).start()

    def y_prev_half(c):
        remote(mine(c, PREV).at[low], r12.at[c, 1, low], y_sent, y_recv.at[c, 1], dev_yp).start()

    def y_second(c):
        arrived(tab.at[c], y_recv.at[c, 0])
        sab[c, 0] = (tab[c, 0].astype(F32) + mine(c, NEXT)[low, :].astype(F32)).astype(BF16)
        remote(sab.at[c, 0], r12.at[c, 0, low], y_sent, y_recv.at[c, 1], dev_yn).start()
        sab[c, 1] = (tab[c, 1].astype(F32) + mine(c, PREV)[high, :].astype(F32)).astype(BF16)
        remote(sab.at[c, 1], r12.at[c, 1, high], y_sent, y_recv.at[c, 1], dev_yp).start()

    def y_total(c):
        arrived(r12.at[c], y_recv.at[c, 1])
        return (mine(c, OWN)[...].astype(F32) + r12[c, 0].astype(F32) + r12[c, 1].astype(F32)).astype(BF16)

    def x_swap(c):
        xs[c] = y_total(c)
        remote(xs.at[c], xr.at[c], y_sent, y_recv.at[c, 2], dev_x).start()

    def group_far(g):
        project(g, FAR)
        for c in chunks(g):
            y_far(c)

    def group_near(g):
        project(g, NEXT)
        for c in chunks(g):
            y_next_half(c)
        project(g, PREV)
        for c in chunks(g):
            y_prev_half(c)

    def group_second(g):
        for c in chunks(g):
            y_second(c)

    def group_swap(g):
        for c in chunks(g):
            x_swap(c)

    def first_far():
        x_take(FAR)
        y_far(0)

    def first_near():
        x_take(NEXT)
        y_next_half(0)
        x_take(PREV)
        y_prev_half(0)

    def x_share(d):
        piece = cf.at[ys[d], kept]
        remote(piece, piece, y_sent, h_recv.at[1, d], dev_x).start()

    def x_shared(d):
        arrived(cf.at[ys[d], given], h_recv.at[1, d])
        to_core(0, d)

    def first_third():
        x_take(OWN)
        cf[ys[OWN], kept, :] = y_total(0)
        piece = cf.at[ys[OWN], kept]
        remote(piece, piece, y_sent, g_recv.at[0, 0], dev_yn).start()
        remote(piece, piece, y_sent, g_recv.at[0, 1], dev_yp).start()
        x_share(OWN)

    def kept_half(h):
        return pl.ds(pl.multiple_of(x_lo * CP + h * HP, HP), HP)

    def first_take():
        arrived(cf.at[ys[PREV], kept], g_recv.at[0, 0])
        x_share(PREV)
        arrived(cf.at[ys[NEXT], kept], g_recv.at[0, 1])
        x_share(NEXT)

    def first_forward():
        piece = cf.at[ys[PREV], kept_half(0)]
        remote(piece, piece, y_sent, g_recv.at[0, 2], dev_yn).start()
        piece = cf.at[ys[NEXT], kept_half(1)]
        remote(piece, piece, y_sent, g_recv.at[0, 2], dev_yp).start()

    def first_last():
        arrived(cf.at[ys[FAR], kept], g_recv.at[0, 2])
        x_share(FAR)

    def to_core(g, d):
        sem = c_recv.at[g] if d == OWN else c_recv.at[NG + d - 1]
        remote(cf.at[ys[d], group(g)], cf.at[ys[d], pl.ds(PL + g * GP, GP)], c_sent, sem, dev_core).start()

    def y_third(g):
        for c in chunks(g):
            arrived(xr.at[c], y_recv.at[c, 2])
            cf[ys[OWN], chunk(c), :] = (xs[c].astype(F32) + xr[c].astype(F32)).astype(BF16)
            piece = cf.at[ys[OWN], chunk(c)]
            remote(piece, piece, y_sent, g_recv.at[g, 0], dev_yn).start()
            remote(piece, piece, y_sent, g_recv.at[g, 1], dev_yp).start()
            there_too = cf.at[ys[OWN], pl.ds(PL + c * CP, CP)]
            remote(piece, there_too, c_sent, c_recv.at[g], dev_core).start()

    def y_take(g):
        arrived(cf.at[ys[PREV], group(g)], g_recv.at[g, 0])
        to_core(g, PREV)
        arrived(cf.at[ys[NEXT], group(g)], g_recv.at[g, 1])
        to_core(g, NEXT)

    def y_forward(g):
        piece = cf.at[ys[PREV], group_half(g, 0)]
        remote(piece, piece, y_sent, g_recv.at[g, 2], dev_yn).start()
        piece = cf.at[ys[NEXT], group_half(g, 1)]
        remote(piece, piece, y_sent, g_recv.at[g, 2], dev_yp).start()

    def y_last(g):
        arrived(cf.at[ys[FAR], group(g)], g_recv.at[g, 2])
        to_core(g, FAR)

    def find_gaps():
        for load in small_loads:
            load.wait()

        def occupied(e, value):
            return jnp.where(occ_ref[...] == e, oe_ref[e], value)

        def empty(e, value):
            return jnp.where(emp_ref[...] == e, ee_ref[e], value)

        zero = jnp.zeros((8, 128), F32)
        below = lax.fori_loop(0, 64, occupied, zero, unroll=8)
        above = lax.fori_loop(0, 256, empty, zero, unroll=8)
        gaps[0] = above - below

    def send_gaps():
        remote(gaps.at[0], gaps.at[1], gap_sent, c_recv.at[NG + 3], dev_core).start()

    def find_factors():
        arrived(gaps.at[1], c_recv.at[NG + 3])
        for n in range(NW):
            frequency = fg_ref[fi_ref[core * NW + n]]
            for src in range(2):
                gap = gaps[src]
                below, above = frequency - gap, frequency + gap
                fac[src, n] = (4.0 / PAIRS) * (
                    below / (below * below + broadening_sq) - above / (above * above + broadening_sq)
                )

    def weigh(g, src):
        if src:
            arrived(cf.at[ys[OWN], pl.ds(PL + g * GP, GP)], c_recv.at[g])
        rows = pl.ds(pl.multiple_of(x_lo * ROWS, ROWS), ROWS)
        for r in range(GP // 128):
            first = src * PL + g * GP + r * 128
            block = cf[ys[OWN], pl.ds(first, 128), rows].astype(F32).T

            def one(n, carry):
                row = fac[src, n, pl.ds(g * (GP // 128) + r, 1), :]
                wt[pl.ds(pl.multiple_of(n * ROWS, ROWS), ROWS), pl.ds(first, 128)] = (
                    block * row
                ).astype(BF16)
                return carry

            lax.fori_loop(0, NW, one, 0, unroll=2)

    turn = [OWN, 3 - 2 * (y % 2), FAR, 1 + 2 * (y % 2)]
    yt = [ys[OWN], (y + 3 - 2 * (y % 2)) % 4, ys[FAR], (y + 1 + 2 * (y % 2)) % 4]
    slot = [yt[d] % 2 for d in range(4)]
    root = [(z % 2) == yt[d] // 2 for d in range(4)]

    def whole(d):
        arrived(cf.at[yt[d], pl.ds(PL, PL)], c_recv.at[NG + turn[d] - 1])

    here, there = pl.ds(0, ROWS), pl.ds(ROWS, ROWS)

    def cols(t):
        return pl.ds(pl.multiple_of((t // 2) * 128, 128), 128)

    def tiles(d, q):
        val[d, q] = jnp.dot(wt[pl.ds(q * QR, QR), :], cf[yt[d]], preferred_element_type=F32)

        @pl.when(root[d])
        def _():
            zo[d, q, 0] = val[d, q, here, cols(z_far)].astype(BF16)
            remote(zo.at[d, q, 0], zt.at[slot[d], q, 0], c_sent, z_recv.at[d, q], dev_zn).start()
            zo[d, q, 1] = val[d, q, there, cols(z_far)].astype(BF16)
            remote(zo.at[d, q, 1], zt.at[slot[d], q, 1], c_sent, z_recv.at[d, q], dev_zp).start()

        @pl.when(jnp.logical_not(root[d]))
        def _():
            zo[d, q, 0] = val[d, q, there, cols(z_next)].astype(BF16)
            remote(zo.at[d, q, 0], zr.at[slot[d], q, 2], c_sent, z_recv.at[d, q], dev_zn).start()
            zo[d, q, 1] = val[d, q, here, cols(z_prev)].astype(BF16)
            remote(zo.at[d, q, 1], zr.at[slot[d], q, 3], c_sent, z_recv.at[d, q], dev_zp).start()

    def z_second(d, q):
        @pl.when(jnp.logical_not(root[d]))
        def _():
            arrived(zt.at[slot[d], q], z_recv.at[d, q])
            zs[slot[d], q, 0] = (val[d, q, here, cols(z_next)] + zt[slot[d], q, 0].astype(F32)).astype(BF16)
            remote(zs.at[slot[d], q, 0], zr.at[slot[d], q, 0], c_sent, z_recv.at[d, q], dev_zn).start()
            zs[slot[d], q, 1] = (val[d, q, there, cols(z_prev)] + zt[slot[d], q, 1].astype(F32)).astype(BF16)
            remote(zs.at[slot[d], q, 1], zr.at[slot[d], q, 1], c_sent, z_recv.at[d, q], dev_zp).start()

    ours = pl.ds(pl.multiple_of(core * 64, 64), 64)
    theirs = pl.ds(pl.multiple_of((1 - core) * 64, 64), 64)

    def z_third(d, q):
        @pl.when(root[d])
        def _():
            arrived(zr.at[slot[d], q], z_recv.at[d, q])

            def total(rows, first, second):
                return (
                    val[d, q, rows, cols(z)]
                    + zr[slot[d], q, first].astype(F32)
                    + zr[slot[d], q, second].astype(F32)
                ).T

            @pl.when(slot[d] == x_hi)
            def _():
                fin[2 * q] = total(here, 0, 3)
                fin[2 * q + 1] = total(there, 2, 1)
                remote(
                    fin.at[pl.ds(2 * q, 2), theirs, :], finr.at[pl.ds(2 * q, 2)], c_sent, x_recv.at[q, 2], dev_core
                ).start()

            @pl.when(slot[d] != x_hi)
            def _():
                zxs[q, 0] = total(here, 0, 3).astype(BF16)
                zxs[q, 1] = total(there, 2, 1).astype(BF16)
                remote(zxs.at[q, :, ours, :], zxr.at[q, 0], c_sent, x_recv.at[q, 0], dev_xh).start()
                remote(zxs.at[q, :, theirs, :], zxr.at[q, 1], c_sent, x_recv.at[q, 1], dev_xhc).start()

    def finish(q):
        arrived(zxr.at[q, 0], x_recv.at[q, 0])
        out_ref[pl.ds(core * NW + 2 * q, 2)] = fin[pl.ds(2 * q, 2), ours, :] + zxr[q, 0].astype(F32)
        arrived(finr.at[pl.ds(2 * q, 2)], x_recv.at[q, 2])
        arrived(zxr.at[q, 1], x_recv.at[q, 1])
        out_ref[pl.ds((1 - core) * NW + 2 * q, 2)] = finr[pl.ds(2 * q, 2)] + zxr[q, 1].astype(F32)

    first_loads()
    project_chunk(2)
    pl.semaphore_wait(barrier, len(peers))
    y_far(2)
    project_chunk(3)
    y_far(3)
    x_give(FAR)
    group_far(2)
    group_near(1)
    x_give(NEXT)
    group_second(1)
    x_give(PREV)
    group_far(3)
    first_far()
    group_near(2)
    group_second(2)
    project(1, OWN)
    first_near()
    group_swap(1)
    x_give(OWN)
    y_second(0)
    group_near(3)
    group_second(3)
    project(2, OWN)
    find_gaps()
    send_gaps()
    y_third(1)
    group_swap(2)
    project(3, OWN)
    first_third()
    group_swap(3)
    find_factors()
    y_third(2)
    weigh(1, 0)
    x_shared(OWN)
    weigh(1, 1)
    weigh(2, 0)
    weigh(0, 0)
    weigh(2, 1)
    y_third(3)
    weigh(3, 0)
    weigh(0, 1)
    first_take()
    first_forward()
    weigh(3, 1)
    tiles(OWN, 0)
    tiles(OWN, 1)
    y_take(1)
    tiles(OWN, 2)
    tiles(OWN, 3)
    x_shared(PREV)
    x_shared(NEXT)
    y_take(2)
    y_forward(1)
    y_take(3)
    y_forward(2)
    y_forward(3)
    z_second(OWN, 0)
    z_second(OWN, 1)
    whole(SECOND)
    tiles(SECOND, 0)
    z_second(OWN, 2)
    tiles(SECOND, 1)
    z_second(OWN, 3)
    tiles(SECOND, 2)
    tiles(SECOND, 3)
    first_last()
    whole(THIRD)
    tiles(THIRD, 0)
    y_last(1)
    z_second(SECOND, 0)
    tiles(THIRD, 1)
    z_second(SECOND, 1)
    y_last(2)
    tiles(THIRD, 2)
    y_last(3)
    tiles(THIRD, 3)
    x_shared(FAR)
    z_second(SECOND, 2)
    z_second(SECOND, 3)
    z_third(OWN, 0)
    z_third(OWN, 1)
    whole(FAR)
    for q in range(NQ):
        tiles(FAR, q)
    for q in range(NQ):
        z_second(THIRD, q)
    for q in range(NQ):
        z_second(FAR, q)
    z_third(OWN, 2)
    z_third(OWN, 3)
    for q in range(NQ):
        z_third(SECOND, q)
    for q in range(NQ):
        z_third(THIRD, q)
    for q in range(NQ):
        z_third(FAR, q)
    for q in range(NQ):
        finish(q)
    arrived(pw.at[pl.ds(0, 896)], y_sent)
    arrived(pw, c_sent)
    arrived(gaps.at[0], gap_sent)


def on_device(pair_waves, subspace_basis, occ_band, empty_band, occ_energy, empty_energy, freq_grid, freq_index):
    vmem = pl.BlockSpec(memory_space=pltpu.VMEM)
    hbm = pl.BlockSpec(memory_space=pltpu.HBM)
    dma = pltpu.SemaphoreType.DMA
    out = pl.pallas_call(
        kernel,
        out_shape=jax.ShapeDtypeStruct((NFREQ, 64, ROWS), F32),
        in_specs=[hbm] * 8,
        out_specs=vmem,
        scratch_shapes=[
            pltpu.VMEM((8, 128), jnp.int32),
            pltpu.VMEM((8, 128), jnp.int32),
            pltpu.SMEM((64,), F32),
            pltpu.SMEM((256,), F32),
            pltpu.SMEM((NFREQ,), F32),
            pltpu.SMEM((NFREQ,), jnp.int32),
            pltpu.VMEM((PL, PWL), BF16),
            pltpu.VMEM((4, PWL, BC), BF16),
            pltpu.VMEM((4, PL, BC), BF16),
            pltpu.VMEM((4, 2 * PL, BC), BF16),
            pltpu.VMEM((NW * ROWS, 2 * PL), BF16),
            pltpu.VMEM((2, 8, 128), F32),
            pltpu.VMEM((2, NW, 8, 128), F32),
            pltpu.VMEM((4, CP, BC), BF16),
            pltpu.VMEM((4, CP, BC), BF16),
            pltpu.VMEM((NC, 2, HP, BC), BF16),
            pltpu.VMEM((NC, 2, HP, BC), BF16),
            pltpu.VMEM((NC, 2, CP, BC), BF16),
            pltpu.VMEM((NC, CP, BC), BF16),
            pltpu.VMEM((NC, CP, BC), BF16),
            pltpu.VMEM((4, NQ, QR, BC), F32),
            pltpu.VMEM((4, NQ, 2, ROWS, ROWS), BF16),
            pltpu.VMEM((2, NQ, 2, ROWS, ROWS), BF16),
            pltpu.VMEM((2, NQ, 2, ROWS, ROWS), BF16),
            pltpu.VMEM((2, NQ, 4, ROWS, ROWS), BF16),
            pltpu.VMEM((NQ, 2, ROWS, ROWS), BF16),
            pltpu.VMEM((NQ, 2, 2, 64, ROWS), BF16),
            pltpu.VMEM((NW, ROWS, ROWS), F32),
            pltpu.VMEM((NW, 64, ROWS), F32),
            dma((NG + 4,)),
            dma((6,)),
            dma((3,)),
            dma((NC, 3)),
            dma((NG, 3)),
            dma((2, 4)),
            dma((4, NQ)),
            dma((NQ, 3)),
            dma((NG + 4,)),
        ],
        compiler_params=pltpu.CompilerParams(collective_id=0, has_side_effects=True, vmem_limit_bytes=48 << 20),
        cost_estimate=pl.CostEstimate(flops=9 << 30, bytes_accessed=9 << 20, transcendentals=0),
    )(
        *(
            pltpu.with_memory_space_constraint(array, pltpu.HBM)
            for array in (
                occ_band.reshape(8, 128), empty_band.reshape(8, 128), pair_waves, subspace_basis,
                occ_energy, empty_energy, freq_grid, freq_index,
            )
        )
    )
    return jnp.swapaxes(out, 1, 2)


def solution(mesh):
    return jax.shard_map(
        on_device,
        mesh=mesh,
        in_specs=(P("pair", "pw"), P("pw", None), P("pair"), P("pair"), P(), P(), P(), P()),
        out_specs=P(None, "pw", "pair"),
        check_vma=False,
    )
```
